32 devices in a mesh: row: 8 (over z, y), col: 4 (over x, core).
Axes of the slice: x: 2, y: 2, z: 4, core: 2. Of those that a mesh axis runs over, the one named last changes fastest.
Arguments:
- tokens: bfloat16 [384, 8192], P('row', 'col'), may hold values from -6 to 6
- weight: bfloat16 [8192, 32768], P('col', 'row'), may hold values from -0.109375 to 0.109375
- tile_rows: int32 [8, 4, 256], P('row', 'col'), may hold values from 0 to 63, as said below
- tile_cols: int32 [8, 4, 256], P('row', 'col'), may hold values from 0 to 255, as said below
- tile_count: int32 [8, 4], P('row', 'col'), may hold values from 64 to 256, as said below
- hidden_cotangent: bfloat16 [384, 32768], P('col', 'row'), may hold values from -6 to 6
Outputs:
- hidden: bfloat16 [384, 32768], P('col', 'row')
- input_grad: bfloat16 [384, 8192], P('row', 'col')
- weight_grad: bfloat16 [8192, 32768], P('col', 'row')
The draws below stay inside these ranges and needn't reach their ends.
Inputs may be any that keep to these rules, and one draw needn't show every extreme that they name: tile_rows[r, c, k] is a row block of the weight (tiles of 128 x 128) among the 16 blocks from c * 16 on, which index c of col holds. tile_cols[r, c, k] is a column block among the 32 blocks from r * 32 on, which index r of row holds; the 256 candidate tiles of one device are distinct. The first tile_count[r, c] candidates of device (r, c) are its nonzero tiles; some device holds 256.
All inputs are finite; a program needn't handle non-finite values.
Results may differ from the reference program's by a relative error of at most 0.0049.
Values may be sent and summed in bfloat16 or wider, within the bound.
A program may use at most 128 MiB of HBM per device.

```python
import jax
import jax.numpy as jnp

D = 8192
FF = 32768
TILE = 128
TOKENS = 384
RBD = 16
CBD = 32
BLOCKS_DEV = 512
CAP = 256
N_ROW = 8
N_COL = 4


def tile_slots(key):
    scores = jax.random.randint(jax.random.fold_in(key, 7), (N_ROW, N_COL, BLOCKS_DEV), 0, 2 ** 20)
    scores = scores * BLOCKS_DEV + jnp.arange(BLOCKS_DEV, dtype=jnp.int32)
    ordering = jnp.argsort(scores, axis=-1, stable=True)
    return ordering[:, :, :CAP].astype(jnp.int32)


def draw_tile_rows(key, part):
    slots = tile_slots(key)
    offset = (jnp.arange(N_COL, dtype=jnp.int32) * RBD)[None, :, None]
    return (offset + slots // CBD).astype(jnp.int32)


def draw_tile_cols(key, part):
    slots = tile_slots(key)
    offset = (jnp.arange(N_ROW, dtype=jnp.int32) * CBD)[:, None, None]
    return (offset + slots % CBD).astype(jnp.int32)


def draw_tile_count(key, part):
    counts = jax.random.randint(jax.random.fold_in(key, 11), (N_ROW, N_COL), CAP // 4, CAP + 1)
    chosen = jax.random.randint(jax.random.fold_in(key, 13), (), 0, N_ROW * N_COL)
    flat_index = jnp.arange(N_ROW * N_COL, dtype=jnp.int32).reshape(N_ROW, N_COL)
    return jnp.where(flat_index == chosen, CAP, counts).astype(jnp.int32)


def steps_of(key, dims, cuts, least, high):
    level = 1.0
    for dim, blocks in cuts:
        steps = jax.random.uniform(jax.random.fold_in(jax.random.fold_in(key, 6), dim), (blocks,), jnp.float32, least / len(cuts), high / len(cuts))
        level = level * jnp.repeat(jnp.exp(steps), dims[dim] // blocks).reshape((-1,) + (1,) * (len(dims) - 1 - dim))
    return level


def noise(rng, dims, width, limit, split=(), kind=jnp.bfloat16):
    array = jax.random.normal(rng, dims, jnp.float32) * width
    if len(split) > 0:
        array = steps_of(rng, dims, split, -0.22, 0.18) * array
    return jnp.clip(array, min=-limit, max=limit).astype(kind)


def setup_inputs(seed: int = 0) -> dict:
    keys = jax.random.split(jax.random.key(seed), 7)
    tokens = noise(keys[0], (TOKENS, D), 1.0, 6.0, ((0, 8), (1, 4)))
    weight = noise(keys[1], (D, FF), (D // 3) ** -0.5, 0.109375, ((0, 4), (1, 8)))
    tile_rows = draw_tile_rows(jax.random.fold_in(keys[6], 71), 0)
    tile_cols = draw_tile_cols(jax.random.fold_in(keys[6], 71), 0)
    tile_count = draw_tile_count(jax.random.fold_in(keys[6], 71), 0)
    hidden_cotangent = noise(keys[5], (TOKENS, FF), 1.0, 6.0, ((0, 4), (1, 8)))
    return dict(tokens=tokens, weight=weight, tile_rows=tile_rows, tile_cols=tile_cols, tile_count=tile_count, hidden_cotangent=hidden_cotangent)


def reference(tokens, weight, tile_rows, tile_cols, tile_count, hidden_cotangent):
    row_list = tile_rows.reshape(-1).astype(jnp.int32)
    col_list = tile_cols.reshape(-1).astype(jnp.int32)
    is_live = (jnp.arange(CAP)[None, :] < tile_count.reshape(-1, 1)).reshape(-1).astype(jnp.float32)
    block_mask = jnp.zeros((D // TILE, FF // TILE), jnp.float32).at[row_list, col_list].max(is_live)
    dense_mask = jnp.repeat(jnp.repeat(block_mask.astype(jnp.bfloat16), TILE, 0), TILE, 1)
    masked = weight * dense_mask
    pre_act = jnp.dot(tokens, masked, preferred_element_type=jnp.float32)
    gate_value = jax.nn.sigmoid(pre_act)
    hidden = (pre_act * gate_value).astype(jnp.bfloat16)
    silu_slope = gate_value * (1.0 + pre_act * (1.0 - gate_value))
    grad_pre = (hidden_cotangent.astype(jnp.float32) * silu_slope).astype(jnp.bfloat16)
    input_grad = jnp.dot(grad_pre, masked.T, preferred_element_type=jnp.float32).astype(jnp.bfloat16)
    full_grad = jnp.dot(tokens.T, grad_pre, preferred_element_type=jnp.float32)
    weight_grad = jnp.where(dense_mask > 0, full_grad, jnp.zeros_like(full_grad)).astype(jnp.bfloat16)
    return hidden, input_grad, weight_grad
```

```python
import functools

import jax
import jax.numpy as jnp
from jax import lax
from jax.experimental import pallas as pl
from jax.experimental.pallas import tpu as pltpu
from jax.sharding import PartitionSpec as P

TILE = 128
SUB = 16
LAG_SUM = 2
LAG_PASS = 4
LAG_BACK = 5
MESH = pl.DeviceIdType.MESH
F32 = jnp.float32
BF16 = jnp.bfloat16


class Plan:
    def __init__(self, n_row, n_col, tokens, weight):
        self.n_row, self.n_col = n_row, n_col
        self.block, self.depth = tokens.shape
        self.wide = weight.shape[1]
        self.line = n_row // 2
        self.chips = n_col // 2
        self.per_owner = n_row // n_col
        self.groups = self.block // SUB
        self.rows = n_row * SUB
        self.slab = self.per_owner * SUB
        self.chunks = 4
        self.cut = self.wide // self.chunks
        self.units = self.groups * self.chunks
        self.halves = 2
        self.part = self.depth // self.halves
        self.step = min(256, self.cut)
        self.row_blocks = self.depth // TILE
        self.col_blocks = self.wide // TILE


def comm_kernel(
    p,
    tokens, weight, tile_rows, tile_cols, count, cot,
    hidden, ingrad, turned_out, grads_out, mask_out,
    w, mask, toks, turned, grads, share, c1s, c1r, keep, c2s, c2r, own, hid, cotv,
    r1s, r1r, rkeep, r2s, r2r, rown, inout,
    w_sem, local_sem, hid_sem,
    ag_send, ag_fwd, ag_recv, c1_send, c1_recv, c2_send, c2_recv, c3_send, c3_recv,
    c4_send, c4_recv, r1_send, r1_recv, r2_send, r2_recv,
):
    row, col = lax.axis_index("row"), lax.axis_index("col")
    pair, line = lax.rem(row, 2), lax.div(row, 2)
    core, chip = lax.rem(col, 2), lax.div(col, 2)
    partner = (line * 2 + 1 - pair, col)
    sibling = (row, chip * 2 + 1 - core)

    def line_peer(step):
        return lax.rem(line + step, p.line)

    def chip_peer(step):
        return lax.rem(chip + step, p.chips)

    def place(block):
        owner = lax.div(block, p.per_owner)
        other = lax.rem(lax.rem(owner, 2) + core, 2)
        slab = other * p.chips + lax.div(owner, 2)
        return pl.multiple_of(slab * p.slab + lax.rem(block, p.per_owner) * SUB, SUB)

    def remote(src, dst, send, recv, device):
        return pltpu.make_async_remote_copy(
            src_ref=src, dst_ref=dst, send_sem=send, recv_sem=recv,
            device_id=device, device_id_type=MESH,
        )

    def load_weight(j):
        return pltpu.make_async_copy(
            weight.at[:, pl.ds(j * p.cut, p.cut)], w.at[j], w_sem.at[j]
        )

    def own_rows(g):
        return tokens.at[pl.ds(pl.multiple_of(g * SUB, SUB), SUB), :]

    def tok_rows(g, block):
        return toks.at[g, pl.ds(place(block), SUB), :]

    def load_own(g):
        return pltpu.make_async_copy(own_rows(g), tok_rows(g, row), local_sem.at[g])

    def ag_line(g, step):
        return remote(
            own_rows(g), tok_rows(g, row), ag_send.at[g, step], ag_recv.at[g, row],
            (line_peer(step) * 2 + pair, col),
        )

    def ag_pair(g):
        return remote(
            own_rows(g), tok_rows(g, row), ag_send.at[g, 0], ag_recv.at[g, row], partner
        )

    def ag_pass(g, step):
        block = line_peer(step) * 2 + pair
        return remote(
            tok_rows(g, block), tok_rows(g, block), ag_fwd.at[g, step], ag_recv.at[g, block],
            partner,
        )

    def ag_arrival(g, block):
        return remote(
            tok_rows(g, block), tok_rows(g, block), ag_send.at[g, 0], ag_recv.at[g, block],
            partner,
        )

    def slab_rows(j, g, index):
        start = pl.multiple_of(g * p.rows + index * p.slab, SUB)
        return grads.at[j, pl.ds(start, p.slab), :]

    def c1_copy(u):
        return remote(c1s.at[u], c1r.at[u], c1_send.at[u], c1_recv.at[u], sibling)

    def c2_copy(u, step):
        return remote(
            c2s.at[u, step], c2r.at[u, step], c2_send.at[u, step], c2_recv.at[u, step],
            (row, chip_peer(step) * 2 + core),
        )

    def c3_copy(u, g, j, step):
        return remote(
            slab_rows(j, g, chip), slab_rows(j, g, chip), c3_send.at[u, step],
            c3_recv.at[u, step], (row, chip_peer(step) * 2 + core),
        )

    def c3_arrival(u, g, j, step):
        source = lax.rem(chip + p.chips - step, p.chips)
        return remote(
            slab_rows(j, g, source), slab_rows(j, g, source), c3_send.at[u, step],
            c3_recv.at[u, step], (row, source * 2 + core),
        )

    def c4_copy(u, g, j, step):
        source = lax.rem(chip + p.chips - step, p.chips)
        return remote(
            slab_rows(j, g, source), slab_rows(j, g, p.chips + source), c4_send.at[u, step],
            c4_recv.at[u, step], sibling,
        )

    def hid_copy(u, g, j, i):
        start = pl.multiple_of(i * p.block + g * SUB, SUB)
        return pltpu.make_async_copy(
            hid.at[u, pl.ds(i * SUB, SUB), :],
            hidden.at[pl.ds(start, SUB), pl.ds(pl.multiple_of(j * p.cut, 128), p.cut)],
            hid_sem.at[u, i],
        )

    def r1_copy(g, h):
        return remote(
            r1s.at[g, h], r1r.at[g, h], r1_send.at[g, h], r1_recv.at[g, h], partner
        )

    def r2_copy(g, h, step):
        return remote(
            r2s.at[g, h, step], r2r.at[g, h, step], r2_send.at[g, h, step],
            r2_recv.at[g, h, step], (line_peer(step) * 2 + pair, col),
        )

    def gather_start(g):
        for step in range(1, p.line):
            ag_line(g, step).start()
        ag_pair(g).start()

    def gather_pass(g):
        for step in range(1, p.line):
            block = line_peer(step) * 2 + pair
            ag_arrival(g, block).wait_recv()
            ag_pass(g, step).start()

    def gather_rest(g):
        for step in range(p.line):
            ag_arrival(g, line_peer(step) * 2 + 1 - pair).wait_recv()

    def mask_chunk(j):
        load_weight(j).wait()
        for block in range(p.row_blocks):
            rows = pl.ds(block * TILE, TILE)
            one = mask[j, pl.ds(block * SUB, SUB), :]
            w[j, rows, :] = w[j, rows, :] * jnp.concatenate([one] * (TILE // SUB), axis=0)

    def forward(u, g, j):
        half = p.rows // 2
        for n in range(p.cut // p.step):
            cols = pl.ds(n * p.step, p.step)
            product = jnp.dot(toks[g], w[j, :, cols], preferred_element_type=F32)
            keep[:, cols] = product[:half]
            c1s[u, :, cols] = product[half:].astype(BF16)
        c1_copy(u).start()

    def pair_sum(u):
        c1_copy(u).wait_recv()
        for step in range(1, p.chips):
            rows = pl.ds(pl.multiple_of(chip_peer(step) * p.slab, SUB), p.slab)
            c2s[u, step] = (keep[rows, :] + c1r[u, rows, :].astype(F32)).astype(BF16)
            c2_copy(u, step).start()
        rows = pl.ds(pl.multiple_of(chip * p.slab, SUB), p.slab)
        own[lax.rem(u, LAG_SUM + 1)] = keep[rows, :] + c1r[u, rows, :].astype(F32)

    def activate(u, g, j):
        for step in range(1, p.chips):
            c2_copy(u, step).wait_recv()
        cols = pl.ds(pl.multiple_of(j * p.cut, 128), p.cut)
        for i in range(p.per_owner):
            rows = pl.ds(i * SUB, SUB)
            pre = own[lax.rem(u, LAG_SUM + 1), rows, :]
            for step in range(1, p.chips):
                pre = pre + c2r[u, step, rows, :].astype(F32)
            gate = jax.nn.sigmoid(pre)
            hid[u, rows, :] = (pre * gate).astype(BF16)
            slope = gate * (1.0 + pre * (1.0 - gate))
            start = pl.multiple_of(i * p.block + g * SUB, SUB)
            back = cotv[pl.ds(start, SUB), cols].astype(F32) * slope
            spot = pl.multiple_of(g * p.rows + chip * p.slab + i * SUB, SUB)
            grads[j, pl.ds(spot, SUB), :] = back.astype(BF16)
        for step in range(1, p.chips):
            c3_copy(u, g, j, step).start()
        c4_copy(u, g, j, 0).start()
        for i in range(p.per_owner):
            hid_copy(u, g, j, i).start()

    def hand_on(u, g, j):
        for step in range(1, p.chips):
            c3_arrival(u, g, j, step).wait_recv()
            c4_copy(u, g, j, step).start()

    def backward(u, g, j):
        for step in range(p.chips):
            c4_copy(u, g, j, step).wait_recv()
        first = (j == 0).astype(F32)
        left = grads[j, pl.ds(pl.multiple_of(g * p.rows, SUB), p.rows), :]
        for h in range(p.halves):
            for n in range(p.part // p.step):
                cols = pl.ds(h * p.part + n * p.step, p.step)
                product = lax.dot_general(
                    left, w[j, cols, :], (((1,), (1,)), ((), ())), preferred_element_type=F32
                )
                share[:, cols] = jnp.where(first > 0.5, 0.0, share[:, cols]) + product

            @pl.when(j == p.chunks - 1)
            def _():
                cols = pl.ds(h * p.part, p.part)
                for k in range(p.line):
                    away = share[pl.ds(place(2 * k + 1 - pair), SUB), cols]
                    r1s[g, h, k * SUB : (k + 1) * SUB, :] = away.astype(BF16)
                r1_copy(g, h).start()
                for k in range(p.line):
                    stay = share[pl.ds(place(2 * k + pair), SUB), cols]
                    rkeep[g, h, k * SUB : (k + 1) * SUB, :] = stay

    def reduce_pair(g, h):
        r1_copy(g, h).wait_recv()
        for step in range(1, p.line):
            rows = pl.ds(pl.multiple_of(line_peer(step) * SUB, SUB), SUB)
            both = rkeep[g, h, rows, :] + r1r[g, h, rows, :].astype(F32)
            r2s[g, h, step] = both.astype(BF16)
            r2_copy(g, h, step).start()
        rows = pl.ds(pl.multiple_of(line * SUB, SUB), SUB)
        rown[g, h] = rkeep[g, h, rows, :] + r1r[g, h, rows, :].astype(F32)

    def reduce_line(g, h):
        total = rown[g, h]
        for step in range(1, p.line):
            r2_copy(g, h, step).wait_recv()
            total = total + r2r[g, h, step].astype(F32)
        inout[g * SUB : (g + 1) * SUB, h * p.part : (h + 1) * p.part] = total.astype(BF16)

    for j in range(p.chunks):
        load_weight(j).start()
    load_cot = pltpu.make_async_copy(cot, cotv, local_sem.at[p.groups])
    for g in range(p.groups):
        load_own(g).start()
    load_cot.start()

    barrier = pltpu.get_barrier_semaphore()
    peers = [partner, sibling]
    peers += [(line_peer(s) * 2 + pair, col) for s in range(1, p.line)]
    peers += [(row, chip_peer(s) * 2 + core) for s in range(1, p.chips)]
    for peer in peers:
        pl.semaphore_signal(barrier, inc=1, device_id=peer, device_id_type=MESH)
    pl.semaphore_wait(barrier, len(peers))
    gather_start(0)

    cap = tile_rows.shape[2]
    local_rows = tile_rows[0] - col * p.row_blocks
    local_cols = tile_cols[0] - row * p.col_blocks
    live = lax.broadcasted_iota(jnp.int32, (1, cap), 1) < count[0, 0]
    local_rows = jnp.where(live, local_rows, -1)
    row_of = lax.broadcasted_iota(jnp.int32, (p.row_blocks * SUB, cap), 0) // SUB
    row_pick = (row_of == local_rows).astype(F32)
    col_of = lax.broadcasted_iota(jnp.int32, (p.col_blocks, cap), 0)
    col_pick = (col_of == local_cols).astype(F32)
    blocks = lax.dot_general(
        row_pick, col_pick, (((1,), (1,)), ((), ())), preferred_element_type=F32
    )
    for j in range(p.chunks):
        lane_of = lax.broadcasted_iota(jnp.int32, (p.col_blocks, p.cut), 1) + j * p.cut
        block_of = lax.broadcasted_iota(jnp.int32, (p.col_blocks, p.cut), 0)
        spread = (lane_of // TILE == block_of).astype(F32)
        mask[j] = jnp.dot(blocks, spread, preferred_element_type=F32).astype(BF16)
    save_mask = pltpu.make_async_copy(mask, mask_out, local_sem.at[p.groups + 1])
    save_mask.start()
    early = p.chunks // 2
    for j in range(early):
        mask_chunk(j)
    gather_pass(0)
    for g in range(1, p.groups):
        gather_start(g)
    for j in range(early, p.chunks):
        mask_chunk(j)
    for g in range(p.groups):
        load_own(g).wait()
    load_cot.wait()

    def place_of(u):
        return lax.div(u, p.chunks), lax.rem(u, p.chunks)

    def tick(t, carry):
        g, j = place_of(t)

        @pl.when(t < p.units)
        def _():
            @pl.when(j == 0)
            def _():
                gather_rest(g)

            forward(t, g, j)

        @pl.when((t < p.units) & (j == 1))
        def _():
            @pl.when(g + 1 < p.groups)
            def _():
                gather_pass(g + 1)

            turned[:, pl.ds(pl.multiple_of(g * p.rows, 128), p.rows)] = toks[g].T

        for lag, stage in ((LAG_SUM, activate), (LAG_PASS, hand_on), (LAG_BACK, backward)):
            u = t - lag

            @pl.when((u >= 0) & (u < p.units))
            def _(u=u, stage=stage):
                stage(u, *place_of(u))

        @pl.when(t < p.units)
        def _():
            pair_sum(t)

        u = t - LAG_BACK - 2

        @pl.when((u >= 0) & (lax.rem(u + p.chunks, p.chunks) == p.chunks - 1))
        def _():
            for h in range(p.halves):
                reduce_pair(lax.div(u, p.chunks), h)

        return carry

    lax.fori_loop(0, p.units + LAG_BACK, tick, 0)

    save_turned = pltpu.make_async_copy(turned, turned_out, local_sem.at[0])
    save_grads = pltpu.make_async_copy(grads, grads_out, local_sem.at[1])
    save_turned.start()
    save_grads.start()
    last = p.groups - 1
    for g in range(last):
        for h in range(p.halves):
            reduce_line(g, h)
    for h in range(p.halves):
        reduce_pair(last, h)
    for h in range(p.halves):
        reduce_line(last, h)
    save_in = pltpu.make_async_copy(inout, ingrad, local_sem.at[2])
    save_in.start()

    def drain(u, carry):
        g, j = place_of(u)
        c1_copy(u).wait_send()
        for step in range(1, p.chips):
            c2_copy(u, step).wait_send()
            c3_copy(u, g, j, step).wait_send()
        for step in range(p.chips):
            c4_copy(u, g, j, step).wait_send()
        for i in range(p.per_owner):
            hid_copy(u, g, j, i).wait()
        return carry

    lax.fori_loop(0, p.units, drain, 0)
    for g in range(p.groups):
        ag_pair(g).wait_send()
        for step in range(1, p.line):
            ag_line(g, step).wait_send()
            ag_pass(g, step).wait_send()
        for h in range(p.halves):
            r1_copy(g, h).wait_send()
            for step in range(1, p.line):
                r2_copy(g, h, step).wait_send()
    save_mask.wait()
    save_turned.wait()
    save_grads.wait()
    save_in.wait()


def communicate(p, tokens, weight, tile_rows, tile_cols, count, cot):
    half = p.rows // 2
    owned = cot.shape[0]
    dma = pltpu.SemaphoreType.DMA
    tokens_all = p.groups * p.rows
    anywhere = pl.BlockSpec(memory_space=pl.ANY)
    vmem = pl.BlockSpec(memory_space=pltpu.VMEM)
    out = lambda *shape: jax.ShapeDtypeStruct(shape, BF16)
    return pl.pallas_call(
        functools.partial(comm_kernel, p),
        in_specs=[
            anywhere, anywhere, vmem, vmem, pl.BlockSpec(memory_space=pltpu.SMEM), anywhere
        ],
        out_specs=[anywhere] * 5,
        out_shape=[
            out(owned, p.wide),
            out(p.block, p.depth),
            out(p.depth, tokens_all),
            out(p.chunks, tokens_all, p.cut),
            out(p.chunks, p.row_blocks * SUB, p.cut),
        ],
        scratch_shapes=[
            pltpu.VMEM((p.chunks, p.depth, p.cut), BF16),
            pltpu.VMEM((p.chunks, p.row_blocks * SUB, p.cut), BF16),
            pltpu.VMEM((p.groups, p.rows, p.depth), BF16),
            pltpu.VMEM((p.depth, tokens_all), BF16),
            pltpu.VMEM((p.chunks, tokens_all, p.cut), BF16),
            pltpu.VMEM((p.rows, p.depth), F32),
            pltpu.VMEM((p.units, half, p.cut), BF16),
            pltpu.VMEM((p.units, half, p.cut), BF16),
            pltpu.VMEM((half, p.cut), F32),
            pltpu.VMEM((p.units, p.chips, p.slab, p.cut), BF16),
            pltpu.VMEM((p.units, p.chips, p.slab, p.cut), BF16),
            pltpu.VMEM((LAG_SUM + 1, p.slab, p.cut), F32),
            pltpu.VMEM((p.units, p.slab, p.cut), BF16),
            pltpu.VMEM((owned, p.wide), BF16),
            pltpu.VMEM((p.groups, p.halves, p.line * SUB, p.part), BF16),
            pltpu.VMEM((p.groups, p.halves, p.line * SUB, p.part), BF16),
            pltpu.VMEM((p.groups, p.halves, p.line * SUB, p.part), F32),
            pltpu.VMEM((p.groups, p.halves, p.line, SUB, p.part), BF16),
            pltpu.VMEM((p.groups, p.halves, p.line, SUB, p.part), BF16),
            pltpu.VMEM((p.groups, p.halves, SUB, p.part), F32),
            pltpu.VMEM((p.block, p.depth), BF16),
            dma((p.chunks,)),
            dma((p.groups + 2,)),
            dma((p.units, p.per_owner)),
            dma((p.groups, p.line)),
            dma((p.groups, p.line)),
            dma((p.groups, p.n_row)),
            dma((p.units,)),
            dma((p.units,)),
            dma((p.units, p.chips)),
            dma((p.units, p.chips)),
            dma((p.units, p.chips)),
            dma((p.units, p.chips)),
            dma((p.units, p.chips)),
            dma((p.units, p.chips)),
            dma((p.groups, p.halves)),
            dma((p.groups, p.halves)),
            dma((p.groups, p.halves, p.line)),
            dma((p.groups, p.halves, p.line)),
        ],
        compiler_params=pltpu.CompilerParams(
            collective_id=0, has_side_effects=True, vmem_limit_bytes=60 * 1024 * 1024
        ),
        name="exchange",
    )(tokens, weight, tile_rows, tile_cols, count, cot)


def weight_kernel(p, turned, grads, mask, hidden_in, ingrad_in, weight_grad, hidden, ingrad):
    hidden[...] = hidden_in[...]
    ingrad[...] = ingrad_in[...]
    for block in range(p.row_blocks):
        rows = pl.ds(block * TILE, TILE)
        product = jnp.dot(turned[rows, :], grads[0], preferred_element_type=F32)
        one = mask[0, pl.ds(block * SUB, SUB), :]
        keep = jnp.concatenate([one] * (TILE // SUB), axis=0)
        weight_grad[rows, :] = product.astype(BF16) * keep


def finish(p, turned, grads, mask, hidden, ingrad):
    width = min(512, p.cut)
    per = p.cut // width
    owned = hidden.shape[0]
    chunked = lambda a: pl.BlockSpec((1, a.shape[1], width), lambda i: (i // per, 0, i % per))
    column = lambda rows: pl.BlockSpec((rows, width), lambda i: (0, i))
    whole = lambda a: pl.BlockSpec(a.shape, lambda i: (0,) * a.ndim)
    shape = jax.ShapeDtypeStruct
    return pl.pallas_call(
        functools.partial(weight_kernel, p),
        grid=(p.wide // width,),
        in_specs=[whole(turned), chunked(grads), chunked(mask), column(owned), whole(ingrad)],
        out_specs=[column(p.depth), column(owned), whole(ingrad)],
        out_shape=[
            shape((p.depth, p.wide), BF16), shape(hidden.shape, BF16), shape(ingrad.shape, BF16)
        ],
        compiler_params=pltpu.CompilerParams(
            dimension_semantics=("arbitrary",), vmem_limit_bytes=48 * 1024 * 1024
        ),
        name="weight_grad",
    )(turned, grads, mask, hidden, ingrad)


def on_device(n_row, n_col, tokens, weight, tile_rows, tile_cols, tile_count, cot):
    p = Plan(n_row, n_col, tokens, weight)
    hidden, ingrad, turned, grads, mask = communicate(
        p, tokens, weight, tile_rows, tile_cols, tile_count, cot
    )
    weight_grad, hidden, ingrad = finish(p, turned, grads, mask, hidden, ingrad)
    return hidden, ingrad, weight_grad


def solution(mesh):
    in_specs = (
        P("row", "col"),
        P("col", "row"),
        P("row", "col", None),
        P("row", "col", None),
        P("row", "col"),
        P("col", "row"),
    )
    out_specs = (P("col", "row"), P("row", "col"), P("col", "row"))
    return jax.shard_map(
        functools.partial(on_device, mesh.shape["row"], mesh.shape["col"]),
        mesh=mesh, in_specs=in_specs, out_specs=out_specs, check_vma=False,
    )
```

```python
import functools

import jax
import jax.numpy as jnp
from jax import lax
from jax.experimental import pallas as pl
from jax.experimental.pallas import tpu as pltpu
from jax.sharding import PartitionSpec as P

TILE = 128
SUB = 16
LAG_SUM = 2
LAG_PASS = 4
LAG_BACK = 5
MESH = pl.DeviceIdType.MESH
F32 = jnp.float32
BF16 = jnp.bfloat16


class Plan:
    def __init__(self, n_row, n_col, tokens, weight):
        self.n_row, self.n_col = n_row, n_col
        self.block, self.depth = tokens.shape
        self.wide = weight.shape[1]
        self.line = n_row // 2
        self.chips = n_col // 2
        self.per_owner = n_row // n_col
        self.groups = self.block // SUB
        self.rows = n_row * SUB
        self.slab = self.per_owner * SUB
        self.chunks = 4
        self.cut = self.wide // self.chunks
        self.units = self.groups * self.chunks
        self.halves = 2
        self.pieces = 2
        self.strip = self.depth // self.pieces
        self.part = self.depth // self.halves
        self.step = min(256, self.cut)
        self.row_blocks = self.depth // TILE
        self.col_blocks = self.wide // TILE


def comm_kernel(
    p,
    tokens, weight, tile_rows, tile_cols, count, cot,
    hidden, ingrad, turned_out, grads_out, mask_out,
    w, mask, toks, turned, grads, share, c1s, c1r, keep, c2s, c2r, own, hid, cotv,
    r1s, r1r, rkeep, r2s, r2r, rown, inout,
    w_sem, local_sem, hid_sem,
    ag_send, ag_fwd, ag_recv, c1_send, c1_recv, c2_send, c2_recv, c3_send, c3_recv,
    c4_send, c4_recv, r1_send, r1_recv, r2_send, r2_recv,
):
    row, col = lax.axis_index("row"), lax.axis_index("col")
    pair, line = lax.rem(row, 2), lax.div(row, 2)
    core, chip = lax.rem(col, 2), lax.div(col, 2)
    partner = (line * 2 + 1 - pair, col)
    sibling = (row, chip * 2 + 1 - core)

    def line_peer(step):
        return lax.rem(line + step, p.line)

    def chip_peer(step):
        return lax.rem(chip + step, p.chips)

    def place(block):
        owner = lax.div(block, p.per_owner)
        other = lax.rem(lax.rem(owner, 2) + core, 2)
        slab = other * p.chips + lax.div(owner, 2)
        return pl.multiple_of(slab * p.slab + lax.rem(block, p.per_owner) * SUB, SUB)

    def remote(src, dst, send, recv, device):
        return pltpu.make_async_remote_copy(
            src_ref=src, dst_ref=dst, send_sem=send, recv_sem=recv,
            device_id=device, device_id_type=MESH,
        )

    def load_weight(j):
        return pltpu.make_async_copy(
            weight.at[:, pl.ds(j * p.cut, p.cut)], w.at[j], w_sem.at[j]
        )

    def own_rows(g):
        return tokens.at[pl.ds(pl.multiple_of(g * SUB, SUB), SUB), :]

    def tok_rows(g, block):
        return toks.at[g, pl.ds(place(block), SUB), :]

    def load_own(g):
        return pltpu.make_async_copy(own_rows(g), tok_rows(g, row), local_sem.at[g])

    def own_piece(g, q):
        rows = pl.ds(pl.multiple_of(g * SUB, SUB), SUB)
        return tokens.at[rows, pl.ds(q * p.strip, p.strip)]

    def tok_piece(g, q, block):
        return toks.at[g, pl.ds(place(block), SUB), pl.ds(q * p.strip, p.strip)]

    def ag_line(g, q, step):
        return remote(
            own_piece(g, q), tok_piece(g, q, row), ag_send.at[g, q, step],
            ag_recv.at[g, q, row], (line_peer(step) * 2 + pair, col),
        )

    def ag_pair(g, q):
        return remote(
            own_piece(g, q), tok_piece(g, q, row), ag_send.at[g, q, 0],
            ag_recv.at[g, q, row], partner,
        )

    def ag_pass(g, q, step):
        block = line_peer(step) * 2 + pair
        return remote(
            tok_piece(g, q, block), tok_piece(g, q, block), ag_fwd.at[g, q, step],
            ag_recv.at[g, q, block], partner,
        )

    def ag_arrival(g, q, block):
        return remote(
            tok_piece(g, q, block), tok_piece(g, q, block), ag_send.at[g, q, 0],
            ag_recv.at[g, q, block], partner,
        )

    def slab_rows(j, g, index):
        start = pl.multiple_of(g * p.rows + index * p.slab, SUB)
        return grads.at[j, pl.ds(start, p.slab), :]

    def c1_copy(u):
        return remote(c1s.at[u], c1r.at[u], c1_send.at[u], c1_recv.at[u], sibling)

    def c2_copy(u, step):
        return remote(
            c2s.at[u, step], c2r.at[u, step], c2_send.at[u, step], c2_recv.at[u, step],
            (row, chip_peer(step) * 2 + core),
        )

    def c3_copy(u, g, j, step):
        return remote(
            slab_rows(j, g, chip), slab_rows(j, g, chip), c3_send.at[u, step],
            c3_recv.at[u, step], (row, chip_peer(step) * 2 + core),
        )

    def c3_arrival(u, g, j, step):
        source = lax.rem(chip + p.chips - step, p.chips)
        return remote(
            slab_rows(j, g, source), slab_rows(j, g, source), c3_send.at[u, step],
            c3_recv.at[u, step], (row, source * 2 + core),
        )

    def c4_copy(u, g, j, step):
        source = lax.rem(chip + p.chips - step, p.chips)
        return remote(
            slab_rows(j, g, source), slab_rows(j, g, p.chips + source), c4_send.at[u, step],
            c4_recv.at[u, step], sibling,
        )

    def hid_copy(u, g, j, i):
        start = pl.multiple_of(i * p.block + g * SUB, SUB)
        return pltpu.make_async_copy(
            hid.at[u, pl.ds(i * SUB, SUB), :],
            hidden.at[pl.ds(start, SUB), pl.ds(pl.multiple_of(j * p.cut, 128), p.cut)],
            hid_sem.at[u, i],
        )

    def r1_copy(g, h):
        return remote(
            r1s.at[g, h], r1r.at[g, h], r1_send.at[g, h], r1_recv.at[g, h], partner
        )

    def r2_copy(g, h, step):
        return remote(
            r2s.at[g, h, step], r2r.at[g, h, step], r2_send.at[g, h, step],
            r2_recv.at[g, h, step], (line_peer(step) * 2 + pair, col),
        )

    def gather_start(g):
        for q in range(p.pieces):
            for step in range(1, p.line):
                ag_line(g, q, step).start()
            ag_pair(g, q).start()

    def gather_pass(g):
        for q in range(p.pieces):
            for step in reversed(range(1, p.line)):
                ag_arrival(g, q, line_peer(step) * 2 + pair).wait_recv()
                ag_pass(g, q, step).start()

    def gather_rest(g):
        for q in range(p.pieces):
            for step in range(p.line):
                ag_arrival(g, q, line_peer(step) * 2 + 1 - pair).wait_recv()

    def mask_chunk(j):
        load_weight(j).wait()
        for block in range(p.row_blocks):
            rows = pl.ds(block * TILE, TILE)
            one = mask[j, pl.ds(block * SUB, SUB), :]
            w[j, rows, :] = w[j, rows, :] * jnp.concatenate([one] * (TILE // SUB), axis=0)

    def forward(u, g, j):
        half = p.rows // 2
        for n in range(p.cut // p.step):
            cols = pl.ds(n * p.step, p.step)
            product = jnp.dot(toks[g], w[j, :, cols], preferred_element_type=F32)
            keep[lax.rem(u, 2), :, cols] = product[:half]
            c1s[u, :, cols] = product[half:].astype(BF16)
        c1_copy(u).start()

    def pair_sum(u):
        c1_copy(u).wait_recv()
        for step in range(1, p.chips):
            rows = pl.ds(pl.multiple_of(chip_peer(step) * p.slab, SUB), p.slab)
            c2s[u, step] = (keep[lax.rem(u, 2), rows, :] + c1r[u, rows, :].astype(F32)).astype(BF16)
            c2_copy(u, step).start()
        rows = pl.ds(pl.multiple_of(chip * p.slab, SUB), p.slab)
        own[lax.rem(u, LAG_SUM + 1)] = keep[lax.rem(u, 2), rows, :] + c1r[u, rows, :].astype(F32)

    def activate(u, g, j):
        for step in range(1, p.chips):
            c2_copy(u, step).wait_recv()
        cols = pl.ds(pl.multiple_of(j * p.cut, 128), p.cut)
        for i in range(p.per_owner):
            rows = pl.ds(i * SUB, SUB)
            pre = own[lax.rem(u, LAG_SUM + 1), rows, :]
            for step in range(1, p.chips):
                pre = pre + c2r[u, step, rows, :].astype(F32)
            gate = jax.nn.sigmoid(pre)
            hid[u, rows, :] = (pre * gate).astype(BF16)
            slope = gate * (1.0 + pre * (1.0 - gate))
            start = pl.multiple_of(i * p.block + g * SUB, SUB)
            back = cotv[pl.ds(start, SUB), cols].astype(F32) * slope
            spot = pl.multiple_of(g * p.rows + chip * p.slab + i * SUB, SUB)
            grads[j, pl.ds(spot, SUB), :] = back.astype(BF16)
        for step in range(1, p.chips):
            c3_copy(u, g, j, step).start()
        c4_copy(u, g, j, 0).start()
        for i in range(p.per_owner):
            hid_copy(u, g, j, i).start()

    def hand_on(u, g, j):
        for step in range(1, p.chips):
            c3_arrival(u, g, j, step).wait_recv()
            c4_copy(u, g, j, step).start()

    def backward(u, g, j):
        for step in range(p.chips):
            c4_copy(u, g, j, step).wait_recv()
        left = grads[j, pl.ds(pl.multiple_of(g * p.rows, SUB), p.rows), :]

        def product(start):
            return lax.dot_general(
                left, w[j, pl.ds(start, TILE), :], (((1,), (1,)), ((), ())),
                preferred_element_type=F32,
            )

        @pl.when(j == 0)
        def _():
            for start in range(0, p.depth, TILE):
                share[:, pl.ds(start, TILE)] = product(start)

        @pl.when((j > 0) & (j < p.chunks - 1))
        def _():
            for start in range(0, p.depth, TILE):
                share[:, pl.ds(start, TILE)] += product(start)

        @pl.when(j == p.chunks - 1)
        def _():
            for h in range(p.halves):
                for start in range(h * p.part, (h + 1) * p.part, TILE):
                    share[:, pl.ds(start, TILE)] += product(start)
                cols = pl.ds(h * p.part, p.part)
                for k in range(p.line):
                    away = share[pl.ds(place(2 * k + 1 - pair), SUB), cols]
                    r1s[g, h, k * SUB : (k + 1) * SUB, :] = away.astype(BF16)
                r1_copy(g, h).start()
                for k in range(p.line):
                    stay = share[pl.ds(place(2 * k + pair), SUB), cols]
                    rkeep[g, h, k * SUB : (k + 1) * SUB, :] = stay

    def reduce_pair(g, h):
        r1_copy(g, h).wait_recv()
        for step in range(1, p.line):
            rows = pl.ds(pl.multiple_of(line_peer(step) * SUB, SUB), SUB)
            both = rkeep[g, h, rows, :] + r1r[g, h, rows, :].astype(F32)
            r2s[g, h, step] = both.astype(BF16)
            r2_copy(g, h, step).start()
        rows = pl.ds(pl.multiple_of(line * SUB, SUB), SUB)
        rown[g, h] = rkeep[g, h, rows, :] + r1r[g, h, rows, :].astype(F32)

    def reduce_line(g, h):
        total = rown[g, h]
        for step in range(1, p.line):
            r2_copy(g, h, step).wait_recv()
            total = total + r2r[g, h, step].astype(F32)
        inout[g * SUB : (g + 1) * SUB, h * p.part : (h + 1) * p.part] = total.astype(BF16)

    for j in range(p.chunks):
        load_weight(j).start()
    load_cot = pltpu.make_async_copy(cot, cotv, local_sem.at[p.groups])
    for g in range(p.groups):
        load_own(g).start()
    load_cot.start()

    barrier = pltpu.get_barrier_semaphore()
    peers = [partner, sibling]
    peers += [(line_peer(s) * 2 + pair, col) for s in range(1, p.line)]
    peers += [(row, chip_peer(s) * 2 + core) for s in range(1, p.chips)]
    for peer in peers:
        pl.semaphore_signal(barrier, inc=1, device_id=peer, device_id_type=MESH)
    pl.semaphore_wait(barrier, len(peers))
    gather_start(0)

    cap = tile_rows.shape[2]
    local_rows = tile_rows[0] - col * p.row_blocks
    local_cols = tile_cols[0] - row * p.col_blocks
    live = lax.broadcasted_iota(jnp.int32, (1, cap), 1) < count[...]
    local_rows = jnp.where(live, local_rows, -1)
    row_of = lax.broadcasted_iota(jnp.int32, (p.row_blocks * SUB, cap), 0) // SUB
    row_pick = (row_of == local_rows).astype(F32)
    col_of = lax.broadcasted_iota(jnp.int32, (p.col_blocks, cap), 0)
    col_pick = (col_of == local_cols).astype(F32)
    blocks = lax.dot_general(
        row_pick, col_pick, (((1,), (1,)), ((), ())), preferred_element_type=F32
    )
    for j in range(p.chunks):
        lane_of = lax.broadcasted_iota(jnp.int32, (p.col_blocks, p.cut), 1) + j * p.cut
        block_of = lax.broadcasted_iota(jnp.int32, (p.col_blocks, p.cut), 0)
        spread = (lane_of // TILE == block_of).astype(F32)
        mask[j] = jnp.dot(blocks, spread, preferred_element_type=F32).astype(BF16)
    save_mask = pltpu.make_async_copy(mask, mask_out, local_sem.at[p.groups + 1])
    save_mask.start()
    mask_chunk(0)
    gather_pass(0)
    for g in range(1, p.groups):
        gather_start(g)
    for g in range(p.groups):
        load_own(g).wait()
    load_cot.wait()

    def place_of(u):
        return lax.div(u, p.chunks), lax.rem(u, p.chunks)

    def tick(t, carry):
        g, j = place_of(t)

        @pl.when(t < p.units)
        def _():
            @pl.when(j == 0)
            def _():
                gather_rest(g)

            @pl.when((g == 0) & (j > 0))
            def _():
                mask_chunk(j)

            forward(t, g, j)

        @pl.when((t < p.units) & (j == 1))
        def _():
            turned[:, pl.ds(pl.multiple_of(g * p.rows, 128), p.rows)] = toks[g].T

        def late(lag, stage):
            u = t - lag

            @pl.when((u >= 0) & (u < p.units))
            def _():
                stage(u, *place_of(u))

        late(1, lambda u, g, j: pair_sum(u))
        late(LAG_PASS, hand_on)
        late(LAG_BACK, backward)
        late(LAG_SUM, activate)

        @pl.when((j == 1) & (g + 1 < p.groups))
        def _():
            gather_pass(g + 1)

        u = t - LAG_BACK - 3

        @pl.when((u >= 0) & (lax.rem(u + p.chunks, p.chunks) == p.chunks - 1))
        def _():
            for h in range(p.halves):
                reduce_pair(lax.div(u, p.chunks), h)

        return carry

    lax.fori_loop(0, p.units, tick, 0)

    pair_sum(p.units - 1)
    for u in range(p.units - LAG_SUM, p.units - 1):
        activate(u, *divmod(u, p.chunks))

    def tail(i, carry):
        @pl.when(i < LAG_PASS)
        def _():
            u = p.units - LAG_PASS + i
            hand_on(u, *place_of(u))

        @pl.when(i == p.chunks)
        def _():
            for h in range(p.halves):
                reduce_pair(p.groups - 2, h)

        u = p.units - LAG_BACK + i
        backward(u, *place_of(u))

        @pl.when(i == 1)
        def _():
            activate(p.units - 1, *divmod(p.units - 1, p.chunks))

        return carry

    lax.fori_loop(0, LAG_BACK, tail, 0)

    save_turned = pltpu.make_async_copy(turned, turned_out, local_sem.at[0])
    save_grads = pltpu.make_async_copy(grads, grads_out, local_sem.at[1])
    save_turned.start()
    save_grads.start()
    last = p.groups - 1
    for h in range(p.halves):
        reduce_pair(last, h)
    for g in range(p.groups):
        for h in range(p.halves):
            reduce_line(g, h)
    save_in = pltpu.make_async_copy(inout, ingrad, local_sem.at[2])
    save_in.start()

    def drain(u, carry):
        g, j = place_of(u)
        c1_copy(u).wait_send()
        for step in range(1, p.chips):
            c2_copy(u, step).wait_send()
            c3_copy(u, g, j, step).wait_send()
        for step in range(p.chips):
            c4_copy(u, g, j, step).wait_send()
        for i in range(p.per_owner):
            hid_copy(u, g, j, i).wait()
        return carry

    lax.fori_loop(0, p.units, drain, 0)
    for g in range(p.groups):
        for q in range(p.pieces):
            ag_pair(g, q).wait_send()
            for step in range(1, p.line):
                ag_line(g, q, step).wait_send()
                ag_pass(g, q, step).wait_send()
        for h in range(p.halves):
            r1_copy(g, h).wait_send()
            for step in range(1, p.line):
                r2_copy(g, h, step).wait_send()
    save_mask.wait()
    save_turned.wait()
    save_grads.wait()
    save_in.wait()


def communicate(p, tokens, weight, tile_rows, tile_cols, count, cot):
    half = p.rows // 2
    owned = cot.shape[0]
    dma = pltpu.SemaphoreType.DMA
    tokens_all = p.groups * p.rows
    anywhere = pl.BlockSpec(memory_space=pl.ANY)
    vmem = pl.BlockSpec(memory_space=pltpu.VMEM)
    out = lambda *shape: jax.ShapeDtypeStruct(shape, BF16)
    return pl.pallas_call(
        functools.partial(comm_kernel, p),
        in_specs=[
            anywhere, anywhere, vmem, vmem, vmem, anywhere
        ],
        out_specs=[anywhere] * 5,
        out_shape=[
            out(owned, p.wide),
            out(p.block, p.depth),
            out(p.depth, tokens_all),
            out(p.chunks, tokens_all, p.cut),
            out(p.chunks, p.row_blocks * SUB, p.cut),
        ],
        scratch_shapes=[
            pltpu.VMEM((p.chunks, p.depth, p.cut), BF16),
            pltpu.VMEM((p.chunks, p.row_blocks * SUB, p.cut), BF16),
            pltpu.VMEM((p.groups, p.rows, p.depth), BF16),
            pltpu.VMEM((p.depth, tokens_all), BF16),
            pltpu.VMEM((p.chunks, tokens_all, p.cut), BF16),
            pltpu.VMEM((p.rows, p.depth), F32),
            pltpu.VMEM((p.units, half, p.cut), BF16),
            pltpu.VMEM((p.units, half, p.cut), BF16),
            pltpu.VMEM((2, half, p.cut), F32),
            pltpu.VMEM((p.units, p.chips, p.slab, p.cut), BF16),
            pltpu.VMEM((p.units, p.chips, p.slab, p.cut), BF16),
            pltpu.VMEM((LAG_SUM + 1, p.slab, p.cut), F32),
            pltpu.VMEM((p.units, p.slab, p.cut), BF16),
            pltpu.VMEM((owned, p.wide), BF16),
            pltpu.VMEM((p.groups, p.halves, p.line * SUB, p.part), BF16),
            pltpu.VMEM((p.groups, p.halves, p.line * SUB, p.part), BF16),
            pltpu.VMEM((p.groups, p.halves, p.line * SUB, p.part), F32),
            pltpu.VMEM((p.groups, p.halves, p.line, SUB, p.part), BF16),
            pltpu.VMEM((p.groups, p.halves, p.line, SUB, p.part), BF16),
            pltpu.VMEM((p.groups, p.halves, SUB, p.part), F32),
            pltpu.VMEM((p.block, p.depth), BF16),
            dma((p.chunks,)),
            dma((p.groups + 2,)),
            dma((p.units, p.per_owner)),
            dma((p.groups, p.pieces, p.line)),
            dma((p.groups, p.pieces, p.line)),
            dma((p.groups, p.pieces, p.n_row)),
            dma((p.units,)),
            dma((p.units,)),
            dma((p.units, p.chips)),
            dma((p.units, p.chips)),
            dma((p.units, p.chips)),
            dma((p.units, p.chips)),
            dma((p.units, p.chips)),
            dma((p.units, p.chips)),
            dma((p.groups, p.halves)),
            dma((p.groups, p.halves)),
            dma((p.groups, p.halves, p.line)),
            dma((p.groups, p.halves, p.line)),
        ],
        compiler_params=pltpu.CompilerParams(
            collective_id=0, has_side_effects=True, vmem_limit_bytes=60 * 1024 * 1024
        ),
        name="exchange",
    )(tokens, weight, tile_rows, tile_cols, count, cot)


def weight_kernel(p, turned, grads, mask, hidden_in, ingrad_in, weight_grad, hidden, ingrad):
    hidden[...] = hidden_in[...]
    ingrad[...] = ingrad_in[...]
    for block in range(p.row_blocks):
        rows = pl.ds(block * TILE, TILE)
        product = jnp.dot(turned[rows, :], grads[0], preferred_element_type=F32)
        one = mask[0, pl.ds(block * SUB, SUB), :]
        keep = jnp.concatenate([one] * (TILE // SUB), axis=0)
        weight_grad[rows, :] = product.astype(BF16) * keep


def finish(p, turned, grads, mask, hidden, ingrad):
    width = min(1024, p.cut)
    per = p.cut // width
    owned = hidden.shape[0]
    chunked = lambda a: pl.BlockSpec((1, a.shape[1], width), lambda i: (i // per, 0, i % per))
    column = lambda rows: pl.BlockSpec((rows, width), lambda i: (0, i))
    whole = lambda a: pl.BlockSpec(a.shape, lambda i: (0,) * a.ndim)
    shape = jax.ShapeDtypeStruct
    return pl.pallas_call(
        functools.partial(weight_kernel, p),
        grid=(p.wide // width,),
        in_specs=[whole(turned), chunked(grads), chunked(mask), column(owned), whole(ingrad)],
        out_specs=[column(p.depth), column(owned), whole(ingrad)],
        out_shape=[
            shape((p.depth, p.wide), BF16), shape(hidden.shape, BF16), shape(ingrad.shape, BF16)
        ],
        compiler_params=pltpu.CompilerParams(
            dimension_semantics=("arbitrary",), vmem_limit_bytes=62 * 1024 * 1024
        ),
        name="weight_grad",
    )(turned, grads, mask, hidden, ingrad)


def on_device(n_row, n_col, tokens, weight, tile_rows, tile_cols, tile_count, cot):
    p = Plan(n_row, n_col, tokens, weight)
    hidden, ingrad, turned, grads, mask = communicate(
        p, tokens, weight, tile_rows, tile_cols, tile_count, cot
    )
    weight_grad, hidden, ingrad = finish(p, turned, grads, mask, hidden, ingrad)
    return hidden, ingrad, weight_grad


def solution(mesh):
    in_specs = (
        P("row", "col"),
        P("col", "row"),
        P("row", "col", None),
        P("row", "col", None),
        P("row", "col"),
        P("col", "row"),
    )
    out_specs = (P("col", "row"), P("row", "col"), P("col", "row"))
    return jax.shard_map(
        functools.partial(on_device, mesh.shape["row"], mesh.shape["col"]),
        mesh=mesh, in_specs=in_specs, out_specs=out_specs, check_vma=False,
    )
```

```python
import functools

import jax
import jax.numpy as jnp
from jax import lax
from jax.experimental import pallas as pl
from jax.experimental.pallas import tpu as pltpu
from jax.sharding import PartitionSpec as P

TILE = 128
SUB = 16
LAG_SUM = 2
LAG_PASS = 4
LAG_BACK = 5
MESH = pl.DeviceIdType.MESH
F32 = jnp.float32
BF16 = jnp.bfloat16


class Plan:
    def __init__(self, n_row, n_col, tokens, weight):
        self.n_row, self.n_col = n_row, n_col
        self.block, self.depth = tokens.shape
        self.wide = weight.shape[1]
        self.line = n_row // 2
        self.chips = n_col // 2
        self.per_owner = n_row // n_col
        self.groups = self.block // SUB
        self.rows = n_row * SUB
        self.slab = self.per_owner * SUB
        self.chunks = 4
        self.cut = self.wide // self.chunks
        self.units = self.groups * self.chunks
        self.halves = 2
        self.pieces = 2
        self.strip = self.depth // self.pieces
        self.part = self.depth // self.halves
        self.step = min(256, self.cut)
        self.row_blocks = self.depth // TILE
        self.col_blocks = self.wide // TILE


def weight_rows(turned, grads, mask, target, block):
    rows = pl.ds(pl.multiple_of(block * TILE, TILE), TILE)
    one = mask[pl.ds(pl.multiple_of(block * SUB, SUB), SUB), :]
    keep = jnp.concatenate([one] * (TILE // SUB), axis=0)
    wide = target.shape[1]
    step = min(512, wide)
    for start in range(0, wide, step):
        cols = slice(start, start + step)
        product = jnp.dot(
            turned[rows, :], grads[:, pl.ds(start, step)], preferred_element_type=F32
        )
        target[rows, pl.ds(start, step)] = product.astype(BF16) * keep[:, cols]


def comm_kernel(
    p,
    tokens, weight, rows_in, cols_in, count_in, cot,
    hidden, ingrad, turned_out, grads_out, mask_out, first_out,
    w, mask, toks, turned, grads, share, c1s, c1r, keep, c2s, c2r, own, hid, cotv,
    r1s, r1r, rkeep, r2s, r2r, rown, inout, tile_rows, tile_cols, count,
    w_sem, local_sem, hid_sem, index_sem,
    ag_send, ag_fwd, ag_recv, c1_send, c1_recv, c2_send, c2_recv, c3_send, c3_recv,
    c4_send, c4_recv, r1_send, r1_recv, r2_send, r2_recv,
):
    row, col = lax.axis_index("row"), lax.axis_index("col")
    pair, line = lax.rem(row, 2), lax.div(row, 2)
    core, chip = lax.rem(col, 2), lax.div(col, 2)
    partner = (line * 2 + 1 - pair, col)
    sibling = (row, chip * 2 + 1 - core)

    def line_peer(step):
        return lax.rem(line + step, p.line)

    def chip_peer(step):
        return lax.rem(chip + step, p.chips)

    def place(block):
        owner = lax.div(block, p.per_owner)
        other = lax.rem(lax.rem(owner, 2) + core, 2)
        slab = other * p.chips + lax.div(owner, 2)
        return pl.multiple_of(slab * p.slab + lax.rem(block, p.per_owner) * SUB, SUB)

    def remote(src, dst, send, recv, device):
        return pltpu.make_async_remote_copy(
            src_ref=src, dst_ref=dst, send_sem=send, recv_sem=recv,
            device_id=device, device_id_type=MESH,
        )

    def load_weight(j):
        return pltpu.make_async_copy(
            weight.at[:, pl.ds(j * p.cut, p.cut)], w.at[j], w_sem.at[j]
        )

    def own_rows(g):
        return tokens.at[pl.ds(pl.multiple_of(g * SUB, SUB), SUB), :]

    def tok_rows(g, block):
        return toks.at[g, pl.ds(place(block), SUB), :]

    def load_own(g):
        return pltpu.make_async_copy(own_rows(g), tok_rows(g, row), local_sem.at[g])

    def own_piece(g, q):
        rows = pl.ds(pl.multiple_of(g * SUB, SUB), SUB)
        return tokens.at[rows, pl.ds(q * p.strip, p.strip)]

    def tok_piece(g, q, block):
        return toks.at[g, pl.ds(place(block), SUB), pl.ds(q * p.strip, p.strip)]

    def ag_line(g, q, step):
        return remote(
            own_piece(g, q), tok_piece(g, q, row), ag_send.at[g, q, step],
            ag_recv.at[g, q, row], (line_peer(step) * 2 + pair, col),
        )

    def ag_pair(g, q):
        return remote(
            own_piece(g, q), tok_piece(g, q, row), ag_send.at[g, q, 0],
            ag_recv.at[g, q, row], partner,
        )

    def ag_pass(g, q, step):
        block = line_peer(step) * 2 + pair
        return remote(
            tok_piece(g, q, block), tok_piece(g, q, block), ag_fwd.at[g, q, step],
            ag_recv.at[g, q, block], partner,
        )

    def ag_arrival(g, q, block):
        return remote(
            tok_piece(g, q, block), tok_piece(g, q, block), ag_send.at[g, q, 0],
            ag_recv.at[g, q, block], partner,
        )

    def slab_rows(j, g, index):
        start = pl.multiple_of(g * p.rows + index * p.slab, SUB)
        return grads.at[j, pl.ds(start, p.slab), :]

    def c1_copy(u):
        return remote(c1s.at[u], c1r.at[u], c1_send.at[u], c1_recv.at[u], sibling)

    def c2_copy(u, step):
        return remote(
            c2s.at[u, step], c2r.at[u, step], c2_send.at[u, step], c2_recv.at[u, step],
            (row, chip_peer(step) * 2 + core),
        )

    def c3_copy(u, g, j, step):
        return remote(
            slab_rows(j, g, chip), slab_rows(j, g, chip), c3_send.at[u, step],
            c3_recv.at[u, step], (row, chip_peer(step) * 2 + core),
        )

    def c3_arrival(u, g, j, step):
        source = lax.rem(chip + p.chips - step, p.chips)
        return remote(
            slab_rows(j, g, source), slab_rows(j, g, source), c3_send.at[u, step],
            c3_recv.at[u, step], (row, source * 2 + core),
        )

    def c4_copy(u, g, j, step):
        source = lax.rem(chip + p.chips - step, p.chips)
        return remote(
            slab_rows(j, g, source), slab_rows(j, g, p.chips + source), c4_send.at[u, step],
            c4_recv.at[u, step], sibling,
        )

    def hid_copy(u, g, j, i):
        start = pl.multiple_of(i * p.block + g * SUB, SUB)
        return pltpu.make_async_copy(
            hid.at[u, pl.ds(i * SUB, SUB), :],
            hidden.at[pl.ds(start, SUB), pl.ds(pl.multiple_of(j * p.cut, 128), p.cut)],
            hid_sem.at[u, i],
        )

    def r1_copy(g, h):
        return remote(
            r1s.at[g, h], r1r.at[g, h], r1_send.at[g, h], r1_recv.at[g, h], partner
        )

    def r2_copy(g, h, step):
        return remote(
            r2s.at[g, h, step], r2r.at[g, h, step], r2_send.at[g, h, step],
            r2_recv.at[g, h, step], (line_peer(step) * 2 + pair, col),
        )

    def gather_start(g):
        for q in range(p.pieces):
            for step in range(1, p.line):
                ag_line(g, q, step).start()
            ag_pair(g, q).start()

    def gather_pass(g):
        for q in range(p.pieces):
            for step in reversed(range(1, p.line)):
                ag_arrival(g, q, line_peer(step) * 2 + pair).wait_recv()
                ag_pass(g, q, step).start()

    def gather_rest(g):
        for q in range(p.pieces):
            for step in range(p.line):
                ag_arrival(g, q, line_peer(step) * 2 + 1 - pair).wait_recv()

    def mask_chunk(j):
        load_weight(j).wait()
        for block in range(p.row_blocks):
            rows = pl.ds(block * TILE, TILE)
            one = mask[j, pl.ds(block * SUB, SUB), :]
            w[j, rows, :] = w[j, rows, :] * jnp.concatenate([one] * (TILE // SUB), axis=0)

    def forward(u, g, j):
        half = p.rows // 2
        for n in range(p.cut // p.step):
            cols = pl.ds(n * p.step, p.step)
            product = jnp.dot(toks[g], w[j, :, cols], preferred_element_type=F32)
            keep[lax.rem(u, 2), :, cols] = product[:half]
            c1s[u, :, cols] = product[half:].astype(BF16)
        c1_copy(u).start()

    def pair_sum(u):
        c1_copy(u).wait_recv()
        for step in range(1, p.chips):
            rows = pl.ds(pl.multiple_of(chip_peer(step) * p.slab, SUB), p.slab)
            c2s[u, step] = (keep[lax.rem(u, 2), rows, :] + c1r[u, rows, :].astype(F32)).astype(BF16)
            c2_copy(u, step).start()
        rows = pl.ds(pl.multiple_of(chip * p.slab, SUB), p.slab)
        own[lax.rem(u, LAG_SUM + 1)] = keep[lax.rem(u, 2), rows, :] + c1r[u, rows, :].astype(F32)

    def activate(u, g, j):
        for step in range(1, p.chips):
            c2_copy(u, step).wait_recv()
        cols = pl.ds(pl.multiple_of(j * p.cut, 128), p.cut)
        for i in range(p.per_owner):
            rows = pl.ds(i * SUB, SUB)
            pre = own[lax.rem(u, LAG_SUM + 1), rows, :]
            for step in range(1, p.chips):
                pre = pre + c2r[u, step, rows, :].astype(F32)
            gate = jax.nn.sigmoid(pre)
            hid[u, rows, :] = (pre * gate).astype(BF16)
            slope = gate * (1.0 + pre * (1.0 - gate))
            start = pl.multiple_of(i * p.block + g * SUB, SUB)
            back = cotv[pl.ds(start, SUB), cols].astype(F32) * slope
            spot = pl.multiple_of(g * p.rows + chip * p.slab + i * SUB, SUB)
            grads[j, pl.ds(spot, SUB), :] = back.astype(BF16)
        for step in range(1, p.chips):
            c3_copy(u, g, j, step).start()
        c4_copy(u, g, j, 0).start()
        for i in range(p.per_owner):
            hid_copy(u, g, j, i).start()

    def hand_on(u, g, j):
        for step in range(1, p.chips):
            c3_arrival(u, g, j, step).wait_recv()
            c4_copy(u, g, j, step).start()

    def backward(u, g, j):
        for step in range(p.chips):
            c4_copy(u, g, j, step).wait_recv()
        left = grads[j, pl.ds(pl.multiple_of(g * p.rows, SUB), p.rows), :]

        def product(start):
            return lax.dot_general(
                left, w[j, pl.ds(start, TILE), :], (((1,), (1,)), ((), ())),
                preferred_element_type=F32,
            )

        @pl.when(j == 0)
        def _():
            for start in range(0, p.depth, TILE):
                share[:, pl.ds(start, TILE)] = product(start)

        @pl.when((j > 0) & (j < p.chunks - 1))
        def _():
            for start in range(0, p.depth, TILE):
                share[:, pl.ds(start, TILE)] += product(start)

        @pl.when(j == p.chunks - 1)
        def _():
            for h in range(p.halves):
                for start in range(h * p.part, (h + 1) * p.part, TILE):
                    share[:, pl.ds(start, TILE)] += product(start)
                cols = pl.ds(h * p.part, p.part)
                for k in range(p.line):
                    away = share[pl.ds(place(2 * k + 1 - pair), SUB), cols]
                    r1s[g, h, k * SUB : (k + 1) * SUB, :] = away.astype(BF16)
                if h:

                    @pl.when(g < p.groups - 1)
                    def _():
                        r1_copy(g, h).start()
                else:
                    r1_copy(g, h).start()
                for k in range(p.line):
                    stay = share[pl.ds(place(2 * k + pair), SUB), cols]
                    rkeep[g, h, k * SUB : (k + 1) * SUB, :] = stay

    def reduce_pair(g, h):
        r1_copy(g, h).wait_recv()
        for step in range(1, p.line):
            rows = pl.ds(pl.multiple_of(line_peer(step) * SUB, SUB), SUB)
            both = rkeep[g, h, rows, :] + r1r[g, h, rows, :].astype(F32)
            r2s[g, h, step] = both.astype(BF16)
            r2_copy(g, h, step).start()
        rows = pl.ds(pl.multiple_of(line * SUB, SUB), SUB)
        rown[g, h] = rkeep[g, h, rows, :] + r1r[g, h, rows, :].astype(F32)

    def first_chunk(part):
        def one_block(block, carry):
            weight_rows(turned, grads.at[0], mask.at[0], w.at[0], block)
            return carry

        each = p.row_blocks // 4
        lax.fori_loop(part * each, (part + 1) * each, one_block, 0)

    def reduce_line(g, h):
        total = rown[g, h]
        for step in range(1, p.line):
            r2_copy(g, h, step).wait_recv()
            total = total + r2r[g, h, step].astype(F32)
        inout[g * SUB : (g + 1) * SUB, h * p.part : (h + 1) * p.part] = total.astype(BF16)

    index_loads = [
        pltpu.make_async_copy(source, target, index_sem.at[i])
        for i, (source, target) in enumerate(
            ((rows_in, tile_rows), (cols_in, tile_cols), (count_in, count))
        )
    ]
    for load in index_loads:
        load.start()
    for j in range(p.chunks):
        load_weight(j).start()
    load_cot = pltpu.make_async_copy(cot, cotv, local_sem.at[p.groups])
    for g in range(p.groups):
        load_own(g).start()
    load_cot.start()

    barrier = pltpu.get_barrier_semaphore()
    peers = [partner, sibling]
    peers += [(line_peer(s) * 2 + pair, col) for s in range(1, p.line)]
    peers += [(row, chip_peer(s) * 2 + core) for s in range(1, p.chips)]
    for peer in peers:
        pl.semaphore_signal(barrier, inc=1, device_id=peer, device_id_type=MESH)
    pl.semaphore_wait(barrier, len(peers))
    gather_start(0)

    for load in index_loads:
        load.wait()
    cap = tile_rows.shape[2]
    local_rows = tile_rows[0] - col * p.row_blocks
    local_cols = tile_cols[0] - row * p.col_blocks
    live = lax.broadcasted_iota(jnp.int32, (1, cap), 1) < count[...]
    local_rows = jnp.where(live, local_rows, -1)
    row_of = lax.broadcasted_iota(jnp.int32, (p.row_blocks * SUB, cap), 0) // SUB
    row_pick = (row_of == local_rows).astype(F32)
    col_of = lax.broadcasted_iota(jnp.int32, (p.col_blocks, cap), 0)
    col_pick = (col_of == local_cols).astype(F32)
    blocks = lax.dot_general(
        row_pick, col_pick, (((1,), (1,)), ((), ())), preferred_element_type=F32
    )
    for j in range(p.chunks):
        lane_of = lax.broadcasted_iota(jnp.int32, (p.col_blocks, p.cut), 1) + j * p.cut
        block_of = lax.broadcasted_iota(jnp.int32, (p.col_blocks, p.cut), 0)
        spread = (lane_of // TILE == block_of).astype(F32)
        mask[j] = jnp.dot(blocks, spread, preferred_element_type=F32).astype(BF16)
    save_mask = pltpu.make_async_copy(mask, mask_out, local_sem.at[p.groups + 1])
    save_mask.start()
    mask_chunk(0)
    gather_pass(0)
    gather_start(1)
    for g in range(p.groups):
        load_own(g).wait()
    load_cot.wait()

    def place_of(u):
        return lax.div(u, p.chunks), lax.rem(u, p.chunks)

    def tick(t, carry):
        g, j = place_of(t)

        @pl.when(t < p.units)
        def _():
            @pl.when(j == 0)
            def _():
                gather_rest(g)

            @pl.when((g == 0) & (j > 0))
            def _():
                mask_chunk(j)

            forward(t, g, j)

        @pl.when((t < p.units) & (j == 1))
        def _():
            turned[:, pl.ds(pl.multiple_of(g * p.rows, 128), p.rows)] = toks[g].T

        def late(lag, stage):
            u = t - lag

            @pl.when((u >= 0) & (u < p.units))
            def _():
                stage(u, *place_of(u))

        late(1, lambda u, g, j: pair_sum(u))
        late(LAG_PASS, hand_on)
        late(LAG_BACK, backward)
        late(LAG_SUM, activate)

        @pl.when((j == 1) & (g + 1 < p.groups))
        def _():
            gather_pass(g + 1)

            @pl.when(g + 2 < p.groups)
            def _():
                gather_start(g + 2)

        u = t - LAG_BACK - 3

        @pl.when((u >= 0) & (lax.rem(u + p.chunks, p.chunks) == p.chunks - 1))
        def _():
            for h in range(p.halves):
                reduce_pair(lax.div(u, p.chunks), h)

        return carry

    lax.fori_loop(0, p.units, tick, 0)

    pair_sum(p.units - 1)
    for u in range(p.units - LAG_SUM, p.units - 1):
        activate(u, *divmod(u, p.chunks))

    def tail(i, carry):
        @pl.when(i < LAG_PASS)
        def _():
            u = p.units - LAG_PASS + i
            hand_on(u, *place_of(u))

        @pl.when(i == p.chunks)
        def _():
            for h in range(p.halves):
                reduce_pair(p.groups - 2, h)

        u = p.units - LAG_BACK + i
        backward(u, *place_of(u))

        @pl.when(i == 1)
        def _():
            activate(p.units - 1, *divmod(p.units - 1, p.chunks))

        return carry

    lax.fori_loop(0, LAG_BACK, tail, 0)

    save_turned = pltpu.make_async_copy(turned, turned_out, local_sem.at[0])
    save_grads = pltpu.make_async_copy(grads, grads_out, local_sem.at[1])
    save_turned.start()
    save_grads.start()
    last = p.groups - 1
    save_first = pltpu.make_async_copy(w.at[0], first_out, local_sem.at[3])
    first_chunk(0)
    first_chunk(1)
    r1_copy(last, 0).wait_send()
    r1_copy(last, 1).start()
    first_chunk(2)
    reduce_pair(last, 0)
    first_chunk(3)
    save_first.start()
    reduce_pair(last, 1)
    for g in range(p.groups):
        for h in range(p.halves):
            reduce_line(g, h)
    save_in = pltpu.make_async_copy(inout, ingrad, local_sem.at[2])
    save_in.start()

    def drain(u, carry):
        g, j = place_of(u)
        c1_copy(u).wait_send()
        for step in range(1, p.chips):
            c2_copy(u, step).wait_send()
            c3_copy(u, g, j, step).wait_send()
        for step in range(p.chips):
            c4_copy(u, g, j, step).wait_send()
        for i in range(p.per_owner):
            hid_copy(u, g, j, i).wait()
        return carry

    lax.fori_loop(0, p.units, drain, 0)
    for g in range(p.groups):
        for q in range(p.pieces):
            ag_pair(g, q).wait_send()
            for step in range(1, p.line):
                ag_line(g, q, step).wait_send()
                ag_pass(g, q, step).wait_send()
        for h in range(p.halves):
            if g < last or h + 1 == p.halves:
                r1_copy(g, h).wait_send()
            for step in range(1, p.line):
                r2_copy(g, h, step).wait_send()
    save_mask.wait()
    save_turned.wait()
    save_grads.wait()
    save_in.wait()
    save_first.wait()


def communicate(p, tokens, weight, tile_rows, tile_cols, count, cot):
    half = p.rows // 2
    owned = cot.shape[0]
    dma = pltpu.SemaphoreType.DMA
    tokens_all = p.groups * p.rows
    anywhere = pl.BlockSpec(memory_space=pl.ANY)
    out = lambda *shape: jax.ShapeDtypeStruct(shape, BF16)
    return pl.pallas_call(
        functools.partial(comm_kernel, p),
        in_specs=[anywhere] * 2 + [pl.BlockSpec(memory_space=pltpu.HBM)] * 3 + [anywhere],
        out_specs=[anywhere] * 6,
        out_shape=[
            out(owned, p.wide),
            out(p.block, p.depth),
            out(p.depth, tokens_all),
            out(p.chunks, tokens_all, p.cut),
            out(p.chunks, p.row_blocks * SUB, p.cut),
            out(p.depth, p.cut),
        ],
        scratch_shapes=[
            pltpu.VMEM((p.chunks, p.depth, p.cut), BF16),
            pltpu.VMEM((p.chunks, p.row_blocks * SUB, p.cut), BF16),
            pltpu.VMEM((p.groups, p.rows, p.depth), BF16),
            pltpu.VMEM((p.depth, tokens_all), BF16),
            pltpu.VMEM((p.chunks, tokens_all, p.cut), BF16),
            pltpu.VMEM((p.rows, p.depth), F32),
            pltpu.VMEM((p.units, half, p.cut), BF16),
            pltpu.VMEM((p.units, half, p.cut), BF16),
            pltpu.VMEM((2, half, p.cut), F32),
            pltpu.VMEM((p.units, p.chips, p.slab, p.cut), BF16),
            pltpu.VMEM((p.units, p.chips, p.slab, p.cut), BF16),
            pltpu.VMEM((LAG_SUM + 1, p.slab, p.cut), F32),
            pltpu.VMEM((p.units, p.slab, p.cut), BF16),
            pltpu.VMEM((owned, p.wide), BF16),
            pltpu.VMEM((p.groups, p.halves, p.line * SUB, p.part), BF16),
            pltpu.VMEM((p.groups, p.halves, p.line * SUB, p.part), BF16),
            pltpu.VMEM((p.groups, p.halves, p.line * SUB, p.part), F32),
            pltpu.VMEM((p.groups, p.halves, p.line, SUB, p.part), BF16),
            pltpu.VMEM((p.groups, p.halves, p.line, SUB, p.part), BF16),
            pltpu.VMEM((p.groups, p.halves, SUB, p.part), F32),
            pltpu.VMEM((p.block, p.depth), BF16),
            pltpu.VMEM(tile_rows.shape, jnp.int32),
            pltpu.VMEM(tile_cols.shape, jnp.int32),
            pltpu.VMEM(count.shape, jnp.int32),
            dma((p.chunks,)),
            dma((p.groups + 2,)),
            dma((p.units, p.per_owner)),
            dma((3,)),
            dma((p.groups, p.pieces, p.line)),
            dma((p.groups, p.pieces, p.line)),
            dma((p.groups, p.pieces, p.n_row)),
            dma((p.units,)),
            dma((p.units,)),
            dma((p.units, p.chips)),
            dma((p.units, p.chips)),
            dma((p.units, p.chips)),
            dma((p.units, p.chips)),
            dma((p.units, p.chips)),
            dma((p.units, p.chips)),
            dma((p.groups, p.halves)),
            dma((p.groups, p.halves)),
            dma((p.groups, p.halves, p.line)),
            dma((p.groups, p.halves, p.line)),
        ],
        compiler_params=pltpu.CompilerParams(
            collective_id=0, has_side_effects=True, vmem_limit_bytes=60 * 1024 * 1024
        ),
        name="exchange",
    )(tokens, weight, tile_rows, tile_cols, count, cot)


def weight_kernel(
    p, turned_in, grads_in, mask_in, first_in, hidden_in, ingrad_in,
    weight_grad, hidden, ingrad,
    turned, grads, mask, first, stage, hid, inout, load_sem, chunk_sem, out_sem, pass_sem,
):
    quarter = p.depth // 4
    blocks = p.row_blocks // 4

    def load(source, target, i):
        return pltpu.make_async_copy(source, target, load_sem.at[i])

    def load_chunk(i):
        return (
            pltpu.make_async_copy(grads_in.at[i], grads.at[i], chunk_sem.at[i, 0]),
            pltpu.make_async_copy(mask_in.at[i], mask.at[i], chunk_sem.at[i, 1]),
        )

    def store(i, q):
        rows = pl.ds(q * quarter, quarter)
        return pltpu.make_async_copy(
            stage.at[i % 2, rows, :],
            weight_grad.at[rows, pl.ds(i * p.cut, p.cut)],
            out_sem.at[i % 2, q],
        )

    load_turned = load(turned_in, turned, 0)
    loads = [
        load(first_in, first, 1), load(hidden_in, hid, 2), load(ingrad_in, inout, 3)
    ]
    passes = [
        pltpu.make_async_copy(first, weight_grad.at[:, pl.ds(0, p.cut)], pass_sem.at[0]),
        pltpu.make_async_copy(hid, hidden, pass_sem.at[1]),
        pltpu.make_async_copy(inout, ingrad, pass_sem.at[2]),
    ]
    load_turned.start()
    for i in range(1, p.chunks):
        for copy in load_chunk(i):
            copy.start()
    for copy in loads:
        copy.start()
    load_turned.wait()
    for i in range(1, p.chunks):
        for copy in load_chunk(i):
            copy.wait()
        for q in range(4):
            if i > 2:
                store(i - 2, q).wait()
            for block in range(q * blocks, (q + 1) * blocks):
                weight_rows(turned, grads.at[i], mask.at[i], stage.at[i % 2], block)
            store(i, q).start()
        if i == 1:
            for came, sent in zip(loads, passes):
                came.wait()
                sent.start()
    for i in range(max(1, p.chunks - 2), p.chunks):
        for q in range(4):
            store(i, q).wait()
    for sent in passes:
        sent.wait()


def finish(p, turned, grads, mask, first, hidden, ingrad):
    anywhere = pl.BlockSpec(memory_space=pl.ANY)
    dma = pltpu.SemaphoreType.DMA
    shape = jax.ShapeDtypeStruct
    vmem = lambda a: pltpu.VMEM(a.shape, BF16)
    return pl.pallas_call(
        functools.partial(weight_kernel, p),
        in_specs=[anywhere] * 6,
        out_specs=[anywhere] * 3,
        out_shape=[
            shape((p.depth, p.wide), BF16), shape(hidden.shape, BF16), shape(ingrad.shape, BF16)
        ],
        scratch_shapes=[
            vmem(turned), vmem(grads), vmem(mask), vmem(first),
            pltpu.VMEM((2, p.depth, p.cut), BF16), vmem(hidden), vmem(ingrad),
            dma((4,)), dma((p.chunks, 2)), dma((2, 4)), dma((3,)),
        ],
        compiler_params=pltpu.CompilerParams(vmem_limit_bytes=62 * 1024 * 1024),
        name="weight_grad",
    )(turned, grads, mask, first, hidden, ingrad)


def on_device(n_row, n_col, tokens, weight, tile_rows, tile_cols, tile_count, cot):
    p = Plan(n_row, n_col, tokens, weight)
    hidden, ingrad, turned, grads, mask, first = communicate(
        p, tokens, weight, tile_rows, tile_cols, tile_count, cot
    )
    weight_grad, hidden, ingrad = finish(p, turned, grads, mask, first, hidden, ingrad)
    return hidden, ingrad, weight_grad


def solution(mesh):
    in_specs = (
        P("row", "col"),
        P("col", "row"),
        P("row", "col", None),
        P("row", "col", None),
        P("row", "col"),
        P("col", "row"),
    )
    out_specs = (P("col", "row"), P("row", "col"), P("col", "row"))
    return jax.shard_map(
        functools.partial(on_device, mesh.shape["row"], mesh.shape["col"]),
        mesh=mesh, in_specs=in_specs, out_specs=out_specs, check_vma=False,
    )
```

```python
import functools

import jax
import jax.numpy as jnp
from jax import lax
from jax.experimental import pallas as pl
from jax.experimental.pallas import tpu as pltpu
from jax.sharding import PartitionSpec as P

TILE = 128
SUB = 16
LAG_SUM = 2
LAG_PASS = 4
LAG_BACK = 5
MESH = pl.DeviceIdType.MESH
F32 = jnp.float32
BF16 = jnp.bfloat16


class Plan:
    def __init__(self, n_row, n_col, tokens, weight):
        self.n_row, self.n_col = n_row, n_col
        self.block, self.depth = tokens.shape
        self.wide = weight.shape[1]
        self.line = n_row // 2
        self.chips = n_col // 2
        self.per_owner = n_row // n_col
        self.groups = self.block // SUB
        self.rows = n_row * SUB
        self.slab = self.per_owner * SUB
        self.chunks = 4
        self.cut = self.wide // self.chunks
        self.units = self.groups * self.chunks
        self.halves = 2
        self.pieces = 2
        self.strip = self.depth // self.pieces
        self.part = self.depth // self.halves
        self.step = min(256, self.cut)
        self.row_blocks = self.depth // TILE
        self.col_blocks = self.wide // TILE


def weight_rows(turned, grads, mask, target, block):
    rows = pl.ds(pl.multiple_of(block * TILE, TILE), TILE)
    one = mask[pl.ds(pl.multiple_of(block * SUB, SUB), SUB), :]
    keep = jnp.concatenate([one] * (TILE // SUB), axis=0)
    wide = target.shape[1]
    step = min(512, wide)
    for start in range(0, wide, step):
        cols = slice(start, start + step)
        product = jnp.dot(
            turned[rows, :], grads[:, pl.ds(start, step)], preferred_element_type=F32
        )
        target[rows, pl.ds(start, step)] = product.astype(BF16) * keep[:, cols]


def comm_kernel(
    p,
    tokens, weight, rows_in, cols_in, count_in, cot,
    hidden, ingrad, turned_out, grads_out, mask_out, first_out,
    w, mask, toks, turned, grads, share, c1s, c1r, keep, c2s, c2r, own, hid, cotv,
    r1s, r1r, rkeep, r2s, r2r, rown, inout, tile_rows, tile_cols, count,
    w_sem, local_sem, hid_sem, index_sem,
    ag_send, ag_fwd, ag_recv, c1_send, c1_recv, c2_send, c2_recv, c3_send, c3_recv,
    c4_send, c4_recv, r1_send, r1_recv, r2_send, r2_recv,
):
    row, col = lax.axis_index("row"), lax.axis_index("col")
    pair, line = lax.rem(row, 2), lax.div(row, 2)
    core, chip = lax.rem(col, 2), lax.div(col, 2)
    partner = (line * 2 + 1 - pair, col)
    sibling = (row, chip * 2 + 1 - core)

    def line_peer(step):
        return lax.rem(line + step, p.line)

    def chip_peer(step):
        return lax.rem(chip + step, p.chips)

    def place(block):
        owner = lax.div(block, p.per_owner)
        other = lax.rem(lax.rem(owner, 2) + core, 2)
        slab = other * p.chips + lax.div(owner, 2)
        return pl.multiple_of(slab * p.slab + lax.rem(block, p.per_owner) * SUB, SUB)

    def remote(src, dst, send, recv, device):
        return pltpu.make_async_remote_copy(
            src_ref=src, dst_ref=dst, send_sem=send, recv_sem=recv,
            device_id=device, device_id_type=MESH,
        )

    def load_weight(j):
        return pltpu.make_async_copy(
            weight.at[:, pl.ds(j * p.cut, p.cut)], w.at[j], w_sem.at[j]
        )

    def own_rows(g):
        return tokens.at[pl.ds(pl.multiple_of(g * SUB, SUB), SUB), :]

    def tok_rows(g, block):
        return toks.at[g, pl.ds(place(block), SUB), :]

    def load_own(g):
        return pltpu.make_async_copy(own_rows(g), tok_rows(g, row), local_sem.at[g])

    def own_piece(g, q):
        rows = pl.ds(pl.multiple_of(g * SUB, SUB), SUB)
        return tokens.at[rows, pl.ds(q * p.strip, p.strip)]

    def tok_piece(g, q, block):
        return toks.at[g, pl.ds(place(block), SUB), pl.ds(q * p.strip, p.strip)]

    def ag_line(g, q, step):
        return remote(
            own_piece(g, q), tok_piece(g, q, row), ag_send.at[g, q, step],
            ag_recv.at[g, q, row], (line_peer(step) * 2 + pair, col),
        )

    def ag_pair(g, q):
        return remote(
            own_piece(g, q), tok_piece(g, q, row), ag_send.at[g, q, 0],
            ag_recv.at[g, q, row], partner,
        )

    def ag_pass(g, q, step):
        block = line_peer(step) * 2 + pair
        return remote(
            tok_piece(g, q, block), tok_piece(g, q, block), ag_fwd.at[g, q, step],
            ag_recv.at[g, q, block], partner,
        )

    def ag_arrival(g, q, block):
        return remote(
            tok_piece(g, q, block), tok_piece(g, q, block), ag_send.at[g, q, 0],
            ag_recv.at[g, q, block], partner,
        )

    def slab_rows(j, g, index):
        start = pl.multiple_of(g * p.rows + index * p.slab, SUB)
        return grads.at[j, pl.ds(start, p.slab), :]

    def c1_copy(u):
        return remote(c1s.at[u], c1r.at[u], c1_send.at[u], c1_recv.at[u], sibling)

    def c2_copy(u, step):
        return remote(
            c2s.at[u, step], c2r.at[u, step], c2_send.at[u, step], c2_recv.at[u, step],
            (row, chip_peer(step) * 2 + core),
        )

    def c3_copy(u, g, j, step):
        return remote(
            slab_rows(j, g, chip), slab_rows(j, g, chip), c3_send.at[u, step],
            c3_recv.at[u, step], (row, chip_peer(step) * 2 + core),
        )

    def c3_arrival(u, g, j, step):
        source = lax.rem(chip + p.chips - step, p.chips)
        return remote(
            slab_rows(j, g, source), slab_rows(j, g, source), c3_send.at[u, step],
            c3_recv.at[u, step], (row, source * 2 + core),
        )

    def c4_copy(u, g, j, step):
        source = lax.rem(chip + p.chips - step, p.chips)
        return remote(
            slab_rows(j, g, source), slab_rows(j, g, p.chips + source), c4_send.at[u, step],
            c4_recv.at[u, step], sibling,
        )

    def hid_copy(u, g, j, i):
        start = pl.multiple_of(i * p.block + g * SUB, SUB)
        return pltpu.make_async_copy(
            hid.at[u, pl.ds(i * SUB, SUB), :],
            hidden.at[pl.ds(start, SUB), pl.ds(pl.multiple_of(j * p.cut, 128), p.cut)],
            hid_sem.at[u, i],
        )

    def r1_copy(g, h):
        return remote(
            r1s.at[g, h], r1r.at[g, h], r1_send.at[g, h], r1_recv.at[g, h], partner
        )

    def r2_copy(g, h, step):
        return remote(
            r2s.at[g, h, step], r2r.at[g, h, step], r2_send.at[g, h, step],
            r2_recv.at[g, h, step], (line_peer(step) * 2 + pair, col),
        )

    def gather_start(g):
        for q in range(p.pieces):
            for step in range(1, p.line):
                ag_line(g, q, step).start()
            ag_pair(g, q).start()

    def gather_pass(g):
        for q in range(p.pieces):
            for step in reversed(range(1, p.line)):
                ag_arrival(g, q, line_peer(step) * 2 + pair).wait_recv()
                ag_pass(g, q, step).start()

    def gather_rest(g):
        for q in range(p.pieces):
            for step in range(p.line):
                ag_arrival(g, q, line_peer(step) * 2 + 1 - pair).wait_recv()

    def mask_chunk(j):
        load_weight(j).wait()
        for block in range(p.row_blocks):
            rows = pl.ds(block * TILE, TILE)
            one = mask[j, pl.ds(block * SUB, SUB), :]
            w[j, rows, :] = w[j, rows, :] * jnp.concatenate([one] * (TILE // SUB), axis=0)

    def forward(u, g, j):
        half = p.rows // 2
        for n in range(p.cut // p.step):
            cols = pl.ds(n * p.step, p.step)
            product = jnp.dot(toks[g], w[j, :, cols], preferred_element_type=F32)
            keep[lax.rem(u, 2), :, cols] = product[:half]
            c1s[u, :, cols] = product[half:].astype(BF16)
        c1_copy(u).start()

    def pair_sum(u):
        c1_copy(u).wait_recv()
        for step in range(1, p.chips):
            rows = pl.ds(pl.multiple_of(chip_peer(step) * p.slab, SUB), p.slab)
            c2s[u, step] = (keep[lax.rem(u, 2), rows, :] + c1r[u, rows, :].astype(F32)).astype(BF16)
            c2_copy(u, step).start()
        rows = pl.ds(pl.multiple_of(chip * p.slab, SUB), p.slab)
        own[lax.rem(u, LAG_SUM + 1)] = keep[lax.rem(u, 2), rows, :] + c1r[u, rows, :].astype(F32)

    def activate(u, g, j):
        for step in range(1, p.chips):
            c2_copy(u, step).wait_recv()
        cols = pl.ds(pl.multiple_of(j * p.cut, 128), p.cut)
        for i in range(p.per_owner):
            rows = pl.ds(i * SUB, SUB)
            pre = own[lax.rem(u, LAG_SUM + 1), rows, :]
            for step in range(1, p.chips):
                pre = pre + c2r[u, step, rows, :].astype(F32)
            gate = jax.nn.sigmoid(pre)
            hid[u, rows, :] = (pre * gate).astype(BF16)
            slope = gate * (1.0 + pre * (1.0 - gate))
            start = pl.multiple_of(i * p.block + g * SUB, SUB)
            back = cotv[pl.ds(start, SUB), cols].astype(F32) * slope
            spot = pl.multiple_of(g * p.rows + chip * p.slab + i * SUB, SUB)
            grads[j, pl.ds(spot, SUB), :] = back.astype(BF16)
        for step in range(1, p.chips):
            c3_copy(u, g, j, step).start()
        c4_copy(u, g, j, 0).start()
        for i in range(p.per_owner):
            hid_copy(u, g, j, i).start()

    def hand_on(u, g, j):
        for step in range(1, p.chips):
            c3_arrival(u, g, j, step).wait_recv()
            c4_copy(u, g, j, step).start()

    def backward(u, g, j):
        for step in range(p.chips):
            c4_copy(u, g, j, step).wait_recv()
        left = grads[j, pl.ds(pl.multiple_of(g * p.rows, SUB), p.rows), :]

        def product(start):
            return lax.dot_general(
                left, w[j, pl.ds(start, TILE), :], (((1,), (1,)), ((), ())),
                preferred_element_type=F32,
            )

        @pl.when(j == 0)
        def _():
            for start in range(0, p.depth, TILE):
                share[:, pl.ds(start, TILE)] = product(start)

        @pl.when((j > 0) & (j < p.chunks - 1))
        def _():
            for start in range(0, p.depth, TILE):
                share[:, pl.ds(start, TILE)] += product(start)

        @pl.when(j == p.chunks - 1)
        def _():
            for h in range(p.halves):
                for start in range(h * p.part, (h + 1) * p.part, TILE):
                    share[:, pl.ds(start, TILE)] += product(start)
                cols = pl.ds(h * p.part, p.part)
                for k in range(p.line):
                    away = share[pl.ds(place(2 * k + 1 - pair), SUB), cols]
                    r1s[g, h, k * SUB : (k + 1) * SUB, :] = away.astype(BF16)
                if h:

                    @pl.when(g < p.groups - 1)
                    def _():
                        r1_copy(g, h).start()
                else:
                    r1_copy(g, h).start()
                for k in range(p.line):
                    stay = share[pl.ds(place(2 * k + pair), SUB), cols]
                    rkeep[g, h, k * SUB : (k + 1) * SUB, :] = stay

    def reduce_pair(g, h):
        r1_copy(g, h).wait_recv()
        for step in range(1, p.line):
            rows = pl.ds(pl.multiple_of(line_peer(step) * SUB, SUB), SUB)
            both = rkeep[g, h, rows, :] + r1r[g, h, rows, :].astype(F32)
            r2s[g, h, step] = both.astype(BF16)
            r2_copy(g, h, step).start()
        rows = pl.ds(pl.multiple_of(line * SUB, SUB), SUB)
        rown[g, h] = rkeep[g, h, rows, :] + r1r[g, h, rows, :].astype(F32)

    def first_chunk(part):
        def one_block(block, carry):
            weight_rows(turned, grads.at[0], mask.at[0], w.at[0], block)
            return carry

        each = p.row_blocks // 4
        lax.fori_loop(part * each, (part + 1) * each, one_block, 0)

    def reduce_line(g, h):
        total = rown[g, h]
        for step in range(1, p.line):
            r2_copy(g, h, step).wait_recv()
            total = total + r2r[g, h, step].astype(F32)
        inout[g * SUB : (g + 1) * SUB, h * p.part : (h + 1) * p.part] = total.astype(BF16)

    index_loads = [
        pltpu.make_async_copy(source, target, index_sem.at[i])
        for i, (source, target) in enumerate(
            ((rows_in, tile_rows), (cols_in, tile_cols), (count_in, count))
        )
    ]
    for load in index_loads:
        load.start()
    for j in range(p.chunks):
        load_weight(j).start()
    load_cot = pltpu.make_async_copy(cot, cotv, local_sem.at[p.groups])
    for g in range(p.groups):
        load_own(g).start()
    load_cot.start()

    barrier = pltpu.get_barrier_semaphore()
    peers = [partner, sibling]
    peers += [(line_peer(s) * 2 + pair, col) for s in range(1, p.line)]
    peers += [(row, chip_peer(s) * 2 + core) for s in range(1, p.chips)]
    for peer in peers:
        pl.semaphore_signal(barrier, inc=1, device_id=peer, device_id_type=MESH)
    pl.semaphore_wait(barrier, len(peers))
    gather_start(0)

    for load in index_loads:
        load.wait()
    cap = tile_rows.shape[2]
    local_rows = tile_rows[0] - col * p.row_blocks
    local_cols = tile_cols[0] - row * p.col_blocks
    live = lax.broadcasted_iota(jnp.int32, (1, cap), 1) < count[...]
    local_rows = jnp.where(live, local_rows, -1)
    row_of = lax.broadcasted_iota(jnp.int32, (p.row_blocks * SUB, cap), 0) // SUB
    row_pick = (row_of == local_rows).astype(F32)
    col_of = lax.broadcasted_iota(jnp.int32, (p.col_blocks, cap), 0)
    col_pick = (col_of == local_cols).astype(F32)
    blocks = lax.dot_general(
        row_pick, col_pick, (((1,), (1,)), ((), ())), preferred_element_type=F32
    )
    for j in range(p.chunks):
        lane_of = lax.broadcasted_iota(jnp.int32, (p.col_blocks, p.cut), 1) + j * p.cut
        block_of = lax.broadcasted_iota(jnp.int32, (p.col_blocks, p.cut), 0)
        spread = (lane_of // TILE == block_of).astype(F32)
        mask[j] = jnp.dot(blocks, spread, preferred_element_type=F32).astype(BF16)
    save_mask = pltpu.make_async_copy(mask, mask_out, local_sem.at[p.groups + 1])
    save_mask.start()
    mask_chunk(0)
    gather_pass(0)
    gather_start(1)
    for g in range(p.groups):
        load_own(g).wait()
    load_cot.wait()

    def place_of(u):
        return lax.div(u, p.chunks), lax.rem(u, p.chunks)

    def tick(t, carry):
        g, j = place_of(t)

        @pl.when(t < p.units)
        def _():
            @pl.when(j == 0)
            def _():
                gather_rest(g)

            @pl.when((g == 0) & (j > 0))
            def _():
                mask_chunk(j)

            forward(t, g, j)

        @pl.when((t < p.units) & (j == 1))
        def _():
            turned[:, pl.ds(pl.multiple_of(g * p.rows, 128), p.rows)] = toks[g].T

        def late(lag, stage):
            u = t - lag

            @pl.when((u >= 0) & (u < p.units))
            def _():
                stage(u, *place_of(u))

        late(1, lambda u, g, j: pair_sum(u))
        late(LAG_PASS, hand_on)
        late(LAG_BACK, backward)
        late(LAG_SUM, activate)

        @pl.when((j == 1) & (g + 1 < p.groups))
        def _():
            gather_pass(g + 1)

            @pl.when(g + 2 < p.groups)
            def _():
                gather_start(g + 2)

        u = t - LAG_BACK - 3

        @pl.when((u >= 0) & (lax.rem(u + p.chunks, p.chunks) == p.chunks - 1))
        def _():
            for h in range(p.halves):
                reduce_pair(lax.div(u, p.chunks), h)

        return carry

    lax.fori_loop(0, p.units, tick, 0)

    pair_sum(p.units - 1)

    def tail(i, carry):
        @pl.when((i > 0) & (i <= LAG_PASS - 1))
        def _():
            u = p.units - LAG_PASS + i
            hand_on(u, *place_of(u))

        @pl.when(i == LAG_PASS)
        def _():
            for h in range(p.halves):
                reduce_pair(p.groups - 2, h)

        u = p.units - LAG_BACK + i
        backward(u, *place_of(u))

        @pl.when(i == 0)
        def _():
            for u in range(p.units - LAG_SUM, p.units - 1):
                activate(u, *divmod(u, p.chunks))
            u = p.units - LAG_PASS
            hand_on(u, *divmod(u, p.chunks))

        @pl.when(i == 1)
        def _():
            activate(p.units - 1, *divmod(p.units - 1, p.chunks))

        return carry

    lax.fori_loop(0, LAG_BACK, tail, 0)

    save_turned = pltpu.make_async_copy(turned, turned_out, local_sem.at[0])
    save_grads = pltpu.make_async_copy(grads, grads_out, local_sem.at[1])
    save_turned.start()
    save_grads.start()
    last = p.groups - 1
    save_first = pltpu.make_async_copy(w.at[0], first_out, local_sem.at[3])
    first_chunk(0)
    first_chunk(1)
    r1_copy(last, 0).wait_send()
    r1_copy(last, 1).start()
    first_chunk(2)
    reduce_pair(last, 0)
    first_chunk(3)
    save_first.start()
    reduce_pair(last, 1)
    for g in range(p.groups):
        for h in range(p.halves):
            reduce_line(g, h)
    save_in = pltpu.make_async_copy(inout, ingrad, local_sem.at[2])
    save_in.start()

    def drain(u, carry):
        g, j = place_of(u)
        c1_copy(u).wait_send()
        for step in range(1, p.chips):
            c2_copy(u, step).wait_send()
            c3_copy(u, g, j, step).wait_send()
        for step in range(p.chips):
            c4_copy(u, g, j, step).wait_send()
        for i in range(p.per_owner):
            hid_copy(u, g, j, i).wait()
        return carry

    lax.fori_loop(0, p.units, drain, 0)
    for g in range(p.groups):
        for q in range(p.pieces):
            ag_pair(g, q).wait_send()
            for step in range(1, p.line):
                ag_line(g, q, step).wait_send()
                ag_pass(g, q, step).wait_send()
        for h in range(p.halves):
            if g < last or h + 1 == p.halves:
                r1_copy(g, h).wait_send()
            for step in range(1, p.line):
                r2_copy(g, h, step).wait_send()
    save_mask.wait()
    save_turned.wait()
    save_grads.wait()
    save_in.wait()
    save_first.wait()


def communicate(p, tokens, weight, tile_rows, tile_cols, count, cot):
    half = p.rows // 2
    owned = cot.shape[0]
    dma = pltpu.SemaphoreType.DMA
    tokens_all = p.groups * p.rows
    anywhere = pl.BlockSpec(memory_space=pl.ANY)
    out = lambda *shape: jax.ShapeDtypeStruct(shape, BF16)
    return pl.pallas_call(
        functools.partial(comm_kernel, p),
        in_specs=[anywhere] * 2 + [pl.BlockSpec(memory_space=pltpu.HBM)] * 3 + [anywhere],
        out_specs=[anywhere] * 6,
        out_shape=[
            out(owned, p.wide),
            out(p.block, p.depth),
            out(p.depth, tokens_all),
            out(p.chunks, tokens_all, p.cut),
            out(p.chunks, p.row_blocks * SUB, p.cut),
            out(p.depth, p.cut),
        ],
        scratch_shapes=[
            pltpu.VMEM((p.chunks, p.depth, p.cut), BF16),
            pltpu.VMEM((p.chunks, p.row_blocks * SUB, p.cut), BF16),
            pltpu.VMEM((p.groups, p.rows, p.depth), BF16),
            pltpu.VMEM((p.depth, tokens_all), BF16),
            pltpu.VMEM((p.chunks, tokens_all, p.cut), BF16),
            pltpu.VMEM((p.rows, p.depth), F32),
            pltpu.VMEM((p.units, half, p.cut), BF16),
            pltpu.VMEM((p.units, half, p.cut), BF16),
            pltpu.VMEM((2, half, p.cut), F32),
            pltpu.VMEM((p.units, p.chips, p.slab, p.cut), BF16),
            pltpu.VMEM((p.units, p.chips, p.slab, p.cut), BF16),
            pltpu.VMEM((LAG_SUM + 1, p.slab, p.cut), F32),
            pltpu.VMEM((p.units, p.slab, p.cut), BF16),
            pltpu.VMEM((owned, p.wide), BF16),
            pltpu.VMEM((p.groups, p.halves, p.line * SUB, p.part), BF16),
            pltpu.VMEM((p.groups, p.halves, p.line * SUB, p.part), BF16),
            pltpu.VMEM((p.groups, p.halves, p.line * SUB, p.part), F32),
            pltpu.VMEM((p.groups, p.halves, p.line, SUB, p.part), BF16),
            pltpu.VMEM((p.groups, p.halves, p.line, SUB, p.part), BF16),
            pltpu.VMEM((p.groups, p.halves, SUB, p.part), F32),
            pltpu.VMEM((p.block, p.depth), BF16),
            pltpu.VMEM(tile_rows.shape, jnp.int32),
            pltpu.VMEM(tile_cols.shape, jnp.int32),
            pltpu.VMEM(count.shape, jnp.int32),
            dma((p.chunks,)),
            dma((p.groups + 2,)),
            dma((p.units, p.per_owner)),
            dma((3,)),
            dma((p.groups, p.pieces, p.line)),
            dma((p.groups, p.pieces, p.line)),
            dma((p.groups, p.pieces, p.n_row)),
            dma((p.units,)),
            dma((p.units,)),
            dma((p.units, p.chips)),
            dma((p.units, p.chips)),
            dma((p.units, p.chips)),
            dma((p.units, p.chips)),
            dma((p.units, p.chips)),
            dma((p.units, p.chips)),
            dma((p.groups, p.halves)),
            dma((p.groups, p.halves)),
            dma((p.groups, p.halves, p.line)),
            dma((p.groups, p.halves, p.line)),
        ],
        compiler_params=pltpu.CompilerParams(
            collective_id=0, has_side_effects=True, vmem_limit_bytes=60 * 1024 * 1024
        ),
        name="exchange",
    )(tokens, weight, tile_rows, tile_cols, count, cot)


def weight_kernel(
    p, turned_in, grads_in, mask_in, first_in, hidden_in, ingrad_in,
    weight_grad, hidden, ingrad,
    turned, grads, mask, first, stage, hid, inout, load_sem, chunk_sem, out_sem, pass_sem,
):
    quarter = p.depth // 4
    blocks = p.row_blocks // 4

    def load(source, target, i):
        return pltpu.make_async_copy(source, target, load_sem.at[i])

    def load_chunk(i):
        return (
            pltpu.make_async_copy(grads_in.at[i], grads.at[i], chunk_sem.at[i, 0]),
            pltpu.make_async_copy(mask_in.at[i], mask.at[i], chunk_sem.at[i, 1]),
        )

    def store(i, q):
        rows = pl.ds(q * quarter, quarter)
        return pltpu.make_async_copy(
            stage.at[i % 2, rows, :],
            weight_grad.at[rows, pl.ds(i * p.cut, p.cut)],
            out_sem.at[i % 2, q],
        )

    load_turned = load(turned_in, turned, 0)
    loads = [
        load(first_in, first, 1), load(hidden_in, hid, 2), load(ingrad_in, inout, 3)
    ]
    passes = [
        pltpu.make_async_copy(first, weight_grad.at[:, pl.ds(0, p.cut)], pass_sem.at[0]),
        pltpu.make_async_copy(hid, hidden, pass_sem.at[1]),
        pltpu.make_async_copy(inout, ingrad, pass_sem.at[2]),
    ]
    load_turned.start()
    for i in range(1, p.chunks):
        for copy in load_chunk(i):
            copy.start()
    for copy in loads:
        copy.start()
    load_turned.wait()
    for i in range(1, p.chunks):
        for copy in load_chunk(i):
            copy.wait()
        for q in range(4):
            if i > 2:
                store(i - 2, q).wait()
            for block in range(q * blocks, (q + 1) * blocks):
                weight_rows(turned, grads.at[i], mask.at[i], stage.at[i % 2], block)
            store(i, q).start()
        if i == 1:
            for came, sent in zip(loads, passes):
                came.wait()
                sent.start()
    for i in range(max(1, p.chunks - 2), p.chunks):
        for q in range(4):
            store(i, q).wait()
    for sent in passes:
        sent.wait()


def finish(p, turned, grads, mask, first, hidden, ingrad):
    anywhere = pl.BlockSpec(memory_space=pl.ANY)
    dma = pltpu.SemaphoreType.DMA
    shape = jax.ShapeDtypeStruct
    vmem = lambda a: pltpu.VMEM(a.shape, BF16)
    return pl.pallas_call(
        functools.partial(weight_kernel, p),
        in_specs=[anywhere] * 6,
        out_specs=[anywhere] * 3,
        out_shape=[
            shape((p.depth, p.wide), BF16), shape(hidden.shape, BF16), shape(ingrad.shape, BF16)
        ],
        scratch_shapes=[
            vmem(turned), vmem(grads), vmem(mask), vmem(first),
            pltpu.VMEM((2, p.depth, p.cut), BF16), vmem(hidden), vmem(ingrad),
            dma((4,)), dma((p.chunks, 2)), dma((2, 4)), dma((3,)),
        ],
        compiler_params=pltpu.CompilerParams(vmem_limit_bytes=62 * 1024 * 1024),
        name="weight_grad",
    )(turned, grads, mask, first, hidden, ingrad)


def on_device(n_row, n_col, tokens, weight, tile_rows, tile_cols, tile_count, cot):
    p = Plan(n_row, n_col, tokens, weight)
    hidden, ingrad, turned, grads, mask, first = communicate(
        p, tokens, weight, tile_rows, tile_cols, tile_count, cot
    )
    weight_grad, hidden, ingrad = finish(p, turned, grads, mask, first, hidden, ingrad)
    return hidden, ingrad, weight_grad


def solution(mesh):
    in_specs = (
        P("row", "col"),
        P("col", "row"),
        P("row", "col", None),
        P("row", "col", None),
        P("row", "col"),
        P("col", "row"),
    )
    out_specs = (P("col", "row"), P("row", "col"), P("col", "row"))
    return jax.shard_map(
        functools.partial(on_device, mesh.shape["row"], mesh.shape["col"]),
        mesh=mesh, in_specs=in_specs, out_specs=out_specs, check_vma=False,
    )
```
